32 devices in a mesh: ctx: 8 (over z, y), tp: 4 (over x, core).
Axes of the slice: x: 2, y: 2, z: 4, core: 2. Of those that a mesh axis runs over, the one named last changes fastest.
Arguments:
- tokens: bfloat16 [2048, 5376], P('ctx', 'tp'), as said below
- out_grad: bfloat16 [2048, 5376], P('ctx', 'tp'), may hold values from -6 to 6
- in_gain: float32 [5376], replicated, may hold values from 0.5 to 1.5
- query_gain: float32 [128], replicated, may hold values from 0.25 to 1.75
- key_gain: float32 [128], replicated, may hold values from 0.25 to 1.75
- post_gain: float32 [5376], replicated, may hold values from 0.5 to 1.5
- q_codes: int32 [5376, 2048], P('ctx', 'tp'), may hold values from 0 to 15
- q_scodes: int32 [5376, 32], P('ctx', 'tp'), may hold values from 0 to 255
- q_second: float32 [21, 32], P(None, 'tp'), as said below
- kv_codes: int32 [2, 5376, 1024], P(None, 'ctx', 'tp'), may hold values from 0 to 15
- kv_scodes: int32 [2, 5376, 16], P(None, 'ctx', 'tp'), may hold values from 0 to 255
- kv_second: float32 [2, 21, 16], P(None, None, 'tp'), as said below
- o_codes: int32 [5376, 2048], P('ctx', 'tp'), may hold values from 0 to 15
- o_scodes: int32 [5376, 32], P('ctx', 'tp'), may hold values from 0 to 255
- o_second: float32 [21, 32], P(None, 'tp'), as said below
- q_down: bfloat16 [5376, 16], replicated, may hold values from -0.078125 to 0.078125
- query_up: bfloat16 [16, 2048], P(None, 'tp'), may hold values from -0.23925781 to 0.23925781
- kv_down: bfloat16 [2, 5376, 16], replicated, may hold values from -0.078125 to 0.078125
- key_value_up: bfloat16 [2, 16, 1024], P(None, None, 'tp'), may hold values from -0.23925781 to 0.23925781
- output_down: bfloat16 [2048, 16], P('tp'), may hold values from -0.125 to 0.125
- output_up: bfloat16 [16, 5376], replicated, may hold values from -0.23925781 to 0.23925781
Outputs:
- mixed: bfloat16 [2048, 5376], P('ctx', 'tp')
- tokens_grad: float32 [2048, 5376], P('ctx', 'tp')
- query_down_gradient: float32 [5376, 16], replicated
- query_up_gradient: float32 [16, 2048], P(None, 'tp')
- key_value_down_gradient: float32 [2, 5376, 16], replicated
- key_value_up_gradient: float32 [2, 16, 1024], P(None, None, 'tp')
- output_down_gradient: float32 [2048, 16], P('tp')
- output_up_gradient: float32 [16, 5376], replicated
- in_projection: float32 [2048, 1], P('ctx')
The draws below stay inside these ranges and needn't reach their ends.
Inputs may be any that keep to these rules, and one draw needn't show every extreme that they name: `q_second`: positive, between one and eight over the square root of 5376. `kv_second`: positive, between one and eight over the square root of 5376. `o_second`: positive, between one and eight over the square root of 2048. `tokens`: real-valued activations of magnitude up to some tens.
All inputs are finite; a program needn't handle non-finite values.
Results may differ from the reference program's by a relative error of at most 0.015.
Values may be sent and summed in bfloat16 or wider, within the bound.
A program may use at most 128 MiB of HBM per device.

```python
import jax
import jax.numpy as jnp
from jax import lax

D = 5376
HEAD_SIZE = 128
HQ = 16
KEY_VALUE_HEADS = 8
RANK = 16
WINDOW_TOKENS = 1024
QBLOCK = 64
QGROUP = 256
SLAB_TOKENS = 2048
FQ = 2048
FK = 1024


def spread_log(key, shape, lowest, highest):
    return jnp.exp(jax.random.uniform(key, shape, jnp.float32, jnp.log(lowest), jnp.log(highest)))


def draw_tokens(key, part):
    streams = jax.random.split(jax.random.fold_in(key, 11), 4)
    row_scales = spread_log(streams[0], (SLAB_TOKENS, 1), 0.3, 3.0)
    column_scales = spread_log(streams[1], (1, D), 0.3, 3.0)
    values = jax.random.normal(streams[3], (SLAB_TOKENS, D), jnp.float32)
    return (values * row_scales * column_scales).astype(jnp.bfloat16)


def scale_table(key, shape, fan_in):
    root = float(fan_in) ** 0.5
    return spread_log(key, shape, 2.0 / root, 5.0 / root)


def draw_q_second(key, part):
    return scale_table(jax.random.fold_in(key, 21), (D // QGROUP, FQ // QBLOCK), D)


def draw_kv_second(key, part):
    return scale_table(jax.random.fold_in(key, 22), (2, D // QGROUP, FK // QBLOCK), D)


def draw_o_second(key, part):
    return scale_table(jax.random.fold_in(key, 23), (D // QGROUP, FQ // QBLOCK), FQ)


def with_ends(array, rng, low, top_value):
    longest = array.shape.index(max(array.shape))
    spots = []
    for shift in (0, 1):
        where = [jax.random.randint(jax.random.fold_in(rng, axis), (), 0, length) for axis, length in enumerate(array.shape)]
        where[longest] = (where[longest] + shift) % array.shape[longest]
        spots.append(tuple(where))
    return array.at[spots[0]].set(low).at[spots[1]].set(top_value)


def block_scale(rng, shape, cuts, smallest, top_value):
    level, own = 1.0, jax.random.fold_in(rng, 6)
    for position, blocks in cuts:
        steps = jnp.exp(jax.random.uniform(jax.random.fold_in(own, position), (blocks,), jnp.float32, smallest / len(cuts), top_value / len(cuts)))
        level = level * jnp.repeat(steps, shape[position] // blocks).reshape([-1 if axis == position else 1 for axis in range(len(shape))])
    return level


def centred(key, dims, scale, reach, cuts=(), kind=jnp.bfloat16):
    level = block_scale(key, dims, cuts, -0.22, 0.18) if cuts else 1.0
    result = jax.random.normal(key, dims, jnp.float32) * scale * level
    return jnp.minimum(jnp.maximum(result, -reach), reach).astype(kind)


def setup_inputs(seed: int = 0) -> dict:
    splits = jax.random.split(jax.random.key(seed), 22)
    return {
        "tokens": draw_tokens(jax.random.fold_in(splits[21], 71), 0),
        "out_grad": centred(splits[1], (SLAB_TOKENS, D), 1.0, 6.0, ((0, 8), (1, 4))),
        "in_gain": jnp.clip(1.0 + 0.1 * jax.random.normal(splits[2], (D,), jnp.float32), 0.5, 1.5),
        "query_gain": jnp.clip(1.0 + 0.15 * jax.random.normal(splits[3], (HEAD_SIZE,), jnp.float32), 0.25, 1.75),
        "key_gain": jnp.clip(1.0 + 0.15 * jax.random.normal(splits[4], (HEAD_SIZE,), jnp.float32), 0.25, 1.75),
        "post_gain": jnp.clip(1.0 + 0.1 * jax.random.normal(splits[5], (D,), jnp.float32), 0.5, 1.5),
        "q_codes": with_ends(jax.random.randint(splits[6], (D, FQ), 0, 16), jax.random.fold_in(splits[6], 1), 0, 15).astype(jnp.int32),
        "q_scodes": with_ends(jax.random.randint(splits[7], (D, FQ // QBLOCK), 0, 256), jax.random.fold_in(splits[7], 1), 0, 255).astype(jnp.int32),
        "q_second": draw_q_second(jax.random.fold_in(splits[21], 71), 0),
        "kv_codes": with_ends(jax.random.randint(splits[9], (2, D, FK), 0, 16), jax.random.fold_in(splits[9], 1), 0, 15).astype(jnp.int32),
        "kv_scodes": with_ends(jax.random.randint(splits[10], (2, D, FK // QBLOCK), 0, 256), jax.random.fold_in(splits[10], 1), 0, 255).astype(jnp.int32),
        "kv_second": draw_kv_second(jax.random.fold_in(splits[21], 71), 0),
        "o_codes": with_ends(jax.random.randint(splits[12], (D, FQ), 0, 16), jax.random.fold_in(splits[12], 1), 0, 15).astype(jnp.int32),
        "o_scodes": with_ends(jax.random.randint(splits[13], (D, FQ // QBLOCK), 0, 256), jax.random.fold_in(splits[13], 1), 0, 255).astype(jnp.int32),
        "o_second": draw_o_second(jax.random.fold_in(splits[21], 71), 0),
        "q_down": centred(splits[15], (D, RANK), D ** -0.5, 0.078125),
        "query_up": centred(splits[16], (RANK, FQ), 0.04, 0.23925781, ((1, 4),)),
        "kv_down": centred(splits[17], (2, D, RANK), D ** -0.5, 0.078125),
        "key_value_up": centred(splits[18], (2, RANK, FK), 0.04, 0.23925781, ((2, 4),)),
        "output_down": centred(splits[19], (FQ, RANK), FQ ** -0.5, 0.125, ((0, 4),)),
        "output_up": centred(splits[20], (RANK, D), 0.04, 0.23925781),
    }


NORMAL_FLOAT = (-1.0, -0.6961928009986877, -0.5250730514526367, -0.39491748809814453, -0.28444138169288635, -0.18477343022823334, -0.09105003625154495, 0.0, 0.07958029955625534, 0.16093020141124725, 0.24611230194568634, 0.33791524171829224, 0.44070982933044434, 0.5626170039176941, 0.7229568362236023, 1.0)
EPSILON = 1e-06
ADAPTER_SCALE = 2.0
SCORE_SCALE = 168.0 ** (-0.5)
ROPE_BASE = 10000.0

def widen(value_rows):
    return lax.optimization_barrier(value_rows).astype(jnp.float32)

def dequantize(codes, scodes, second):
    height, width = codes.shape
    levels = jnp.zeros(codes.shape, jnp.float32)
    for level in range(16):
        levels = jnp.where(codes == level, jnp.float32(NORMAL_FLOAT[level]), levels)
    second_rows = jnp.repeat(second, QGROUP, axis=0)
    absmax = second_rows * ((scodes.astype(jnp.float32) + 1.0) / 256.0)
    scaled = levels.reshape(height, width // QBLOCK, QBLOCK) * absmax[:, :, None]
    return scaled.reshape(height, width).astype(jnp.bfloat16)

def rope_tables(positions):
    half = HEAD_SIZE // 2
    exponent = jnp.arange(half, dtype=jnp.float32) * (2.0 / HEAD_SIZE)
    frequency = jnp.power(jnp.float32(ROPE_BASE), -exponent)
    angle = positions.astype(jnp.float32)[:, None] * frequency[None, :]
    return (jnp.cos(angle), jnp.sin(angle))

def rotate(heads, cosine, sine):
    half = heads.shape[-1] // 2
    first = heads[..., :half]
    second = heads[..., half:]
    across = cosine[:, None, :]
    along = sine[:, None, :]
    return jnp.concatenate([first * across - second * along, second * across + first * along], axis=-1)

def unrotate(grad, cosine, sine):
    half = grad.shape[-1] // 2
    first = grad[..., :half]
    second = grad[..., half:]
    across = cosine[:, None, :]
    along = sine[:, None, :]
    return jnp.concatenate([first * across + second * along, second * across - first * along], axis=-1)

def head_norm(heads, gain):
    scale = lax.rsqrt(lax.optimization_barrier(jnp.mean(heads * heads, axis=-1, keepdims=True)) + EPSILON)
    return (heads * scale * gain, scale)

def head_norm_back(heads, scale, gain, grad):
    weighted = grad * gain
    inner = lax.optimization_barrier(jnp.mean(weighted * heads, axis=-1, keepdims=True))
    return scale * weighted - scale ** 3 * heads * inner

def probabilities(q_rot, keys, query_pos, key_pos):
    count, q_heads, width = q_rot.shape
    kv_heads = keys.shape[1]
    grouped = q_rot.reshape(count, kv_heads, q_heads // kv_heads, width)
    scores = jnp.einsum('tkgd,lkd->kgtl', widen(grouped), widen(keys)) * SCORE_SCALE
    gap = query_pos[:, None] - key_pos[None, :]
    allowed = (gap >= 0) & (gap < WINDOW_TOKENS) & (key_pos[None, :] >= 0)
    weights = jnp.where(allowed, jnp.exp(scores), 0.0)
    return (weights / lax.optimization_barrier(jnp.sum(weights, axis=-1, keepdims=True)), grouped)

def attention_forward(q_rot, keys, values, query_pos, key_pos):
    count, q_heads, width = q_rot.shape
    probability, grouped = probabilities(q_rot, keys, query_pos, key_pos)
    prob_low = probability.astype(jnp.bfloat16)
    mixed = jnp.einsum('kgtl,lkd->tkgd', widen(prob_low), widen(values))
    return mixed.reshape(count, q_heads * width).astype(jnp.bfloat16)

def attention_backward(q_rot, keys, values, output_gradient, query_pos, key_pos):
    count, q_heads, width = q_rot.shape
    kv_heads = keys.shape[1]
    probability, grouped = probabilities(q_rot, keys, query_pos, key_pos)
    prob_low = probability.astype(jnp.bfloat16)
    grad_grouped = output_gradient.reshape(count, kv_heads, q_heads // kv_heads, width)
    grad_prob = jnp.einsum('tkgd,lkd->kgtl', widen(grad_grouped), widen(values))
    grad_values = jnp.einsum('kgtl,tkgd->lkd', widen(prob_low), widen(grad_grouped))
    inner = lax.optimization_barrier(jnp.sum(probability * grad_prob, axis=-1, keepdims=True))
    grad_scores = (probability * (grad_prob - inner) * SCORE_SCALE).astype(jnp.bfloat16)
    grad_query = jnp.einsum('kgtl,lkd->tkgd', widen(grad_scores), widen(keys)).reshape(count, q_heads, width)
    grad_keys = jnp.einsum('kgtl,tkgd->lkd', widen(grad_scores), widen(grouped))
    return (grad_query, grad_keys, grad_values)

def reference(tokens, out_grad, in_gain, query_gain, key_gain, post_gain, q_codes, q_scodes, q_second, kv_codes, kv_scodes, kv_second, o_codes, o_scodes, o_second, q_down, query_up, kv_down, key_value_up, output_down, output_up):
    query_matrix = dequantize(q_codes, q_scodes, q_second)
    key_matrix = dequantize(kv_codes[0], kv_scodes[0], kv_second[0])
    value_matrix = dequantize(kv_codes[1], kv_scodes[1], kv_second[1])
    output_matrix = dequantize(o_codes, o_scodes, o_second)
    wide = tokens.astype(jnp.float32)
    row_scale = lax.rsqrt(lax.optimization_barrier(jnp.mean(wide * wide, axis=1, keepdims=True)) + EPSILON)
    normalized_input = (wide * row_scale * in_gain).astype(jnp.bfloat16)
    query_lowrank = jnp.dot(normalized_input, q_down, preferred_element_type=jnp.float32).astype(jnp.bfloat16)
    key_lowrank = jnp.dot(normalized_input, kv_down[0], preferred_element_type=jnp.float32).astype(jnp.bfloat16)
    value_lowrank = jnp.dot(normalized_input, kv_down[1], preferred_element_type=jnp.float32).astype(jnp.bfloat16)
    query_rows = jnp.dot(normalized_input, query_matrix, preferred_element_type=jnp.float32) + ADAPTER_SCALE * jnp.dot(query_lowrank, query_up, preferred_element_type=jnp.float32)
    key = jnp.dot(normalized_input, key_matrix, preferred_element_type=jnp.float32) + ADAPTER_SCALE * jnp.dot(key_lowrank, key_value_up[0], preferred_element_type=jnp.float32)
    value_total = jnp.dot(normalized_input, value_matrix, preferred_element_type=jnp.float32) + ADAPTER_SCALE * jnp.dot(value_lowrank, key_value_up[1], preferred_element_type=jnp.float32)
    value_rows = value_total.astype(jnp.bfloat16).reshape(SLAB_TOKENS, KEY_VALUE_HEADS, HEAD_SIZE)
    positions = jnp.arange(SLAB_TOKENS, dtype=jnp.int32)
    cosine, sine = rope_tables(positions)
    q_heads = query_rows.reshape(SLAB_TOKENS, HQ, HEAD_SIZE)
    q_normed, q_scale = head_norm(q_heads, query_gain)
    q_rot = rotate(q_normed, cosine, sine).astype(jnp.bfloat16)
    key_head_rows = key.reshape(SLAB_TOKENS, KEY_VALUE_HEADS, HEAD_SIZE)
    k_normed, k_scale = head_norm(key_head_rows, key_gain)
    k_rot = rotate(k_normed, cosine, sine).astype(jnp.bfloat16)
    front_rows = jnp.zeros((WINDOW_TOKENS, KEY_VALUE_HEADS, HEAD_SIZE), jnp.bfloat16)
    key_pad = jnp.concatenate([front_rows, k_rot], axis=0)
    value_pad = jnp.concatenate([front_rows, value_rows], axis=0)
    blocks = SLAB_TOKENS // WINDOW_TOKENS
    block_ids = jnp.arange(blocks, dtype=jnp.int32)

    def block_inputs(index):
        start = index * WINDOW_TOKENS
        q_block = lax.dynamic_slice_in_dim(q_rot, start, WINDOW_TOKENS, 0)
        k_block = lax.dynamic_slice_in_dim(key_pad, start, 2 * WINDOW_TOKENS, 0)
        v_block = lax.dynamic_slice_in_dim(value_pad, start, 2 * WINDOW_TOKENS, 0)
        query_pos = start + jnp.arange(WINDOW_TOKENS, dtype=jnp.int32)
        key_pos = start - WINDOW_TOKENS + jnp.arange(2 * WINDOW_TOKENS, dtype=jnp.int32)
        return (start, q_block, k_block, v_block, query_pos, key_pos)

    def forward_block(index):
        start, q_block, k_block, v_block, query_pos, key_pos = block_inputs(index)
        return attention_forward(q_block, k_block, v_block, query_pos, key_pos)
    attended_rows = lax.map(forward_block, block_ids).reshape(SLAB_TOKENS, FQ)
    output_lowrank = jnp.dot(attended_rows, output_down, preferred_element_type=jnp.float32).astype(jnp.bfloat16)
    output_total_sum = jnp.dot(attended_rows, output_matrix.T, preferred_element_type=jnp.float32) + ADAPTER_SCALE * jnp.dot(output_lowrank, output_up, preferred_element_type=jnp.float32)
    out_scale = lax.rsqrt(lax.optimization_barrier(jnp.mean(output_total_sum * output_total_sum, axis=1, keepdims=True)) + EPSILON)
    mixed = (wide + output_total_sum * out_scale * post_gain).astype(jnp.bfloat16)
    weighted_out = out_grad.astype(jnp.float32) * post_gain
    out_inner = lax.optimization_barrier(jnp.mean(weighted_out * output_total_sum, axis=1, keepdims=True))
    output_gradient = (out_scale * weighted_out - out_scale ** 3 * output_total_sum * out_inner).astype(jnp.bfloat16)
    output_mixture = jnp.dot(output_gradient, output_up.T, preferred_element_type=jnp.float32).astype(jnp.bfloat16)
    output_up_gradient = ADAPTER_SCALE * jnp.dot(output_lowrank.T, output_gradient, preferred_element_type=jnp.float32)
    output_down_gradient = ADAPTER_SCALE * jnp.dot(attended_rows.T, output_mixture, preferred_element_type=jnp.float32)
    attended_gradient = (jnp.dot(output_gradient, output_matrix, preferred_element_type=jnp.float32) + ADAPTER_SCALE * jnp.dot(output_mixture, output_down.T, preferred_element_type=jnp.float32)).astype(jnp.bfloat16)

    def backward_block(carry, index):
        key_grad, value_grad = carry
        start, q_block, k_block, v_block, query_pos, key_pos = block_inputs(index)
        grad_block = lax.dynamic_slice_in_dim(attended_gradient, start, WINDOW_TOKENS, 0)
        grad_query, grad_keys, grad_values = attention_backward(q_block, k_block, v_block, grad_block, query_pos, key_pos)
        key_grad = lax.dynamic_update_slice_in_dim(key_grad, lax.dynamic_slice_in_dim(key_grad, start, 2 * WINDOW_TOKENS, 0) + grad_keys, start, 0)
        value_grad = lax.dynamic_update_slice_in_dim(value_grad, lax.dynamic_slice_in_dim(value_grad, start, 2 * WINDOW_TOKENS, 0) + grad_values, start, 0)
        return ((key_grad, value_grad), grad_query)
    empty_state = jnp.zeros((SLAB_TOKENS + WINDOW_TOKENS, KEY_VALUE_HEADS, HEAD_SIZE), jnp.float32)
    (key_grad, value_grad), query_grad = lax.scan(backward_block, (empty_state, empty_state), block_ids)
    query_grad = query_grad.reshape(SLAB_TOKENS, HQ, HEAD_SIZE)
    key_grad = key_grad[WINDOW_TOKENS:]
    value_grad = value_grad[WINDOW_TOKENS:]
    q_norm_grad = unrotate(query_grad, cosine, sine)
    k_norm_grad = unrotate(key_grad, cosine, sine)
    query_gradient_lowrank = head_norm_back(q_heads, q_scale, query_gain, q_norm_grad).reshape(SLAB_TOKENS, FQ).astype(jnp.bfloat16)
    key_gradient_lowrank = head_norm_back(key_head_rows, k_scale, key_gain, k_norm_grad).reshape(SLAB_TOKENS, FK).astype(jnp.bfloat16)
    value_gradient_lowrank = value_grad.reshape(SLAB_TOKENS, FK).astype(jnp.bfloat16)
    query_mixture = jnp.dot(query_gradient_lowrank, query_up.T, preferred_element_type=jnp.float32).astype(jnp.bfloat16)
    key_mixture = jnp.dot(key_gradient_lowrank, key_value_up[0].T, preferred_element_type=jnp.float32).astype(jnp.bfloat16)
    value_mixture = jnp.dot(value_gradient_lowrank, key_value_up[1].T, preferred_element_type=jnp.float32).astype(jnp.bfloat16)
    normalized_gradient = jnp.dot(query_gradient_lowrank, query_matrix.T, preferred_element_type=jnp.float32)
    normalized_gradient = normalized_gradient + jnp.dot(key_gradient_lowrank, key_matrix.T, preferred_element_type=jnp.float32)
    normalized_gradient = normalized_gradient + jnp.dot(value_gradient_lowrank, value_matrix.T, preferred_element_type=jnp.float32)
    adapter_term = jnp.dot(query_mixture, q_down.T, preferred_element_type=jnp.float32) + jnp.dot(key_mixture, kv_down[0].T, preferred_element_type=jnp.float32) + jnp.dot(value_mixture, kv_down[1].T, preferred_element_type=jnp.float32)
    normalized_gradient = normalized_gradient + ADAPTER_SCALE * adapter_term
    weighted_in = normalized_gradient * in_gain
    in_inner = lax.optimization_barrier(jnp.mean(weighted_in * wide, axis=1, keepdims=True))
    tokens_grad = out_grad.astype(jnp.float32) + row_scale * weighted_in - row_scale ** 3 * wide * in_inner
    in_projection = float(D) ** 0.5 * row_scale * in_inner
    query_down_gradient = ADAPTER_SCALE * jnp.dot(normalized_input.T, query_mixture, preferred_element_type=jnp.float32)
    key_value_down_gradient = jnp.stack([ADAPTER_SCALE * jnp.dot(normalized_input.T, key_mixture, preferred_element_type=jnp.float32), ADAPTER_SCALE * jnp.dot(normalized_input.T, value_mixture, preferred_element_type=jnp.float32)])
    query_up_gradient = ADAPTER_SCALE * jnp.dot(query_lowrank.T, query_gradient_lowrank, preferred_element_type=jnp.float32)
    key_value_up_gradient = jnp.stack([ADAPTER_SCALE * jnp.dot(key_lowrank.T, key_gradient_lowrank, preferred_element_type=jnp.float32), ADAPTER_SCALE * jnp.dot(value_lowrank.T, value_gradient_lowrank, preferred_element_type=jnp.float32)])
    return (mixed, tokens_grad, query_down_gradient, query_up_gradient, key_value_down_gradient, key_value_up_gradient, output_down_gradient, output_up_gradient, in_projection)
```

```python
import functools

import jax
import jax.numpy as jnp
from jax import lax
from jax.experimental import pallas as pl
from jax.experimental.pallas import tpu as pltpu
from jax.sharding import PartitionSpec as P

D = 5376
HEAD_SIZE = 128
WINDOW_TOKENS = 1024
QBLOCK = 64
QGROUP = 256


NORMAL_FLOAT = (
    -1.0,
    -0.6961928009986877,
    -0.5250730514526367,
    -0.39491748809814453,
    -0.28444138169288635,
    -0.18477343022823334,
    -0.09105003625154495,
    0.0,
    0.07958029955625534,
    0.16093020141124725,
    0.24611230194568634,
    0.33791524171829224,
    0.44070982933044434,
    0.5626170039176941,
    0.7229568362236023,
    1.0,
)
EPSILON = 1e-06
ADAPTER_SCALE = 2.0
SCORE_SCALE = 168.0 ** (-0.5)
ROPE_BASE = 10000.0


def from_behind(shard, axis, by):
    devices = lax.axis_size(axis)
    pairs = [(i, i + by) for i in range(devices) if 0 <= i + by < devices]
    return lax.ppermute(shard, axis, pairs)


MESH = pl.DeviceIdType.MESH


def ring_place(index, devices):
    odd = index % 2
    return (1 - odd) * (index // 2) + odd * (devices - 1 - index // 2)


def ring_index(place, devices):
    back = place // (devices // 2)
    return (1 - back) * 2 * place + back * (2 * (devices - 1 - place) + 1)


def gather_kernel(devices, chunks, a_ref, b_ref, a_out, b_out, own_sem, send_sem, recv_sem):
    me = lax.axis_index("ctx")
    place = ring_place(me, devices)
    right = ring_index((place + 1) % devices, devices)
    left = ring_index((place + devices - 1) % devices, devices)
    barrier = pltpu.get_barrier_semaphore()
    for neighbour in (left, right):
        pl.semaphore_signal(barrier, inc=1, device_id={"ctx": neighbour}, device_id_type=MESH)
    pl.semaphore_wait(barrier, 2)
    own = []
    for way, (source, target) in enumerate(((a_ref, a_out), (b_ref, b_out))):
        own.append(pltpu.make_async_copy(source, target.at[me], own_sem.at[way]))
        own[-1].start()
    rows = a_ref.shape[0] // chunks
    copies = {}
    for step in range(devices - 1):
        for chunk in range(chunks):
            part = pl.ds(chunk * rows, rows)
            for way, (source, target) in enumerate(((a_ref, a_out), (b_ref, b_out))):
                if step > 0:
                    copies[step - 1, chunk, way].wait_recv()
                shift = devices - step if way == 0 else step
                owner = ring_index((place + shift) % devices, devices)
                copy = pltpu.make_async_remote_copy(
                    src_ref=source.at[part] if step == 0 else target.at[owner, part],
                    dst_ref=target.at[owner, part],
                    send_sem=send_sem.at[way, step * chunks + chunk],
                    recv_sem=recv_sem.at[way, step * chunks + chunk],
                    device_id={"ctx": right if way == 0 else left},
                    device_id_type=MESH,
                )
                copy.start()
                copies[step, chunk, way] = copy
    for chunk in range(chunks):
        for way in range(2):
            copies[devices - 2, chunk, way].wait_recv()
    for copy in copies.values():
        copy.wait_send()
    for copy in own:
        copy.wait()


def gather_pair(a, b, collective_id):
    devices = lax.axis_size("ctx")
    rows = a.shape[0]
    chunks = 3 if rows % 48 == 0 else 1
    count = (devices - 1) * chunks
    sent = (devices - 1) * (a.size + b.size) * 2
    gathered = pl.pallas_call(
        functools.partial(gather_kernel, devices, chunks),
        out_shape=[jax.ShapeDtypeStruct((devices,) + x.shape, x.dtype) for x in (a, b)],
        in_specs=[pl.BlockSpec(memory_space=pl.ANY)] * 2,
        out_specs=[pl.BlockSpec(memory_space=pl.ANY)] * 2,
        scratch_shapes=[
            pltpu.SemaphoreType.DMA((2,)),
            pltpu.SemaphoreType.DMA((2, count)),
            pltpu.SemaphoreType.DMA((2, count)),
        ],
        cost_estimate=pl.CostEstimate(flops=0, bytes_accessed=sent * 20, transcendentals=0),
        compiler_params=pltpu.CompilerParams(collective_id=collective_id, has_side_effects=True),
    )(a, b)
    return [x.reshape(devices * rows, x.shape[2]) for x in gathered]


def reduce_kernel(
    devices, sharers, split, g_ref, down_ref, up_ref, slots, summed, gathered, sems, side_sems
):
    me = lax.axis_index("ctx")
    side = lax.axis_index("tp")
    rows = g_ref.shape[0] // devices
    barrier = pltpu.get_barrier_semaphore()
    for k in range(1, devices):
        pl.semaphore_signal(
            barrier, inc=1, device_id={"ctx": (me + k) % devices}, device_id_type=MESH
        )
    for k in range(1, sharers):
        pl.semaphore_signal(
            barrier, inc=1, device_id={"tp": (side + k) % sharers}, device_id_type=MESH
        )
    pl.semaphore_wait(barrier, devices + sharers - 2)
    first = []
    for k in range(1, devices):
        other = (me + k) % devices
        copy = pltpu.make_async_remote_copy(
            src_ref=g_ref.at[pl.ds(pl.multiple_of(other * rows, rows), rows)],
            dst_ref=slots.at[k],
            send_sem=sems.at[0, k],
            recv_sem=sems.at[1, k],
            device_id={"ctx": other},
            device_id_type=MESH,
        )
        copy.start()
        first.append(copy)
    total = g_ref[pl.ds(pl.multiple_of(me * rows, rows), rows), :]
    for k in range(1, devices):
        first[k - 1].wait_recv()
        total = total + slots[k]
    summed[...] = total
    gathered[me] = total
    second = []
    for k in range(1, devices):
        copy = pltpu.make_async_remote_copy(
            src_ref=summed,
            dst_ref=gathered.at[me],
            send_sem=sems.at[2, k],
            recv_sem=sems.at[3, k],
            device_id={"ctx": (me + k) % devices},
            device_id_type=MESH,
        )
        copy.start()
        second.append(copy)
    for copy in second:
        copy.wait_recv()
    third = []
    for k in range(1, sharers):
        copy = pltpu.make_async_remote_copy(
            src_ref=gathered.at[:, :, pl.ds(0, split)],
            dst_ref=down_ref.at[side],
            send_sem=side_sems.at[0, k],
            recv_sem=side_sems.at[1, k],
            device_id={"tp": (side + k) % sharers},
            device_id_type=MESH,
        )
        copy.start()
        third.append(copy)
    down_ref[side] = gathered[:, :, :split]
    up_ref[...] = gathered[:, :, split:]
    for copy in first + second:
        copy.wait_send()
    for copy in third:
        copy.wait()


def reduce_gradients(down, up, collective_id):
    devices = lax.axis_size("ctx")
    sharers = lax.axis_size("tp")
    height, width = down.shape
    up_shape = up.shape
    if height % (8 * devices) or up.size % (128 * height):
        down, up = lax.psum((down, up), "ctx")
        return lax.all_gather(down, "tp"), up
    up = up.reshape(height, up.size // height)
    split = -(-width // 128) * 128
    packed = jnp.concatenate([down, jnp.zeros((height, split - width), jnp.float32), up], axis=1)
    rows = height // devices
    whole = packed.shape[1]
    down, up = pl.pallas_call(
        functools.partial(reduce_kernel, devices, sharers, split),
        out_shape=[
            jax.ShapeDtypeStruct((sharers, devices, rows, split), jnp.float32),
            jax.ShapeDtypeStruct((devices, rows, whole - split), jnp.float32),
        ],
        in_specs=[pl.BlockSpec(memory_space=pltpu.VMEM)],
        out_specs=[pl.BlockSpec(memory_space=pltpu.VMEM)] * 2,
        scratch_shapes=[
            pltpu.VMEM((devices, rows, whole), jnp.float32),
            pltpu.VMEM((rows, whole), jnp.float32),
            pltpu.VMEM((devices, rows, whole), jnp.float32),
            pltpu.SemaphoreType.DMA((4, devices)),
            pltpu.SemaphoreType.DMA((2, sharers)),
        ],
        compiler_params=pltpu.CompilerParams(collective_id=collective_id, has_side_effects=True),
    )(packed)
    return down.reshape(sharers, height, split)[:, :, :width], up.reshape(up_shape)


def dequantize(codes, scodes, second, row_start):
    height, width = codes.shape
    levels = jnp.zeros(codes.shape, jnp.float32)
    for level in range(16):
        levels = jnp.where(codes == level, jnp.float32(NORMAL_FLOAT[level]), levels)
    group_ids = (row_start + jnp.arange(height, dtype=jnp.int32)) // QGROUP
    group_list = jnp.arange(second.shape[0], dtype=jnp.int32)
    picker = (group_ids[:, None] == group_list[None, :]).astype(jnp.float32)
    second_rows = jnp.dot(picker, second, precision=lax.Precision.HIGHEST)
    absmax = second_rows * ((scodes.astype(jnp.float32) + 1.0) / 256.0)
    scaled = levels.reshape(height, width // QBLOCK, QBLOCK) * absmax[:, :, None]
    return scaled.reshape(height, width).astype(jnp.bfloat16)


def rope_tables(positions):
    half = HEAD_SIZE // 2
    exponent = jnp.arange(half, dtype=jnp.float32) * (2.0 / HEAD_SIZE)
    frequency = jnp.power(jnp.float32(ROPE_BASE), -exponent)
    angle = positions.astype(jnp.float32)[:, None] * frequency[None, :]
    return (jnp.cos(angle), jnp.sin(angle))


def rotate(heads, cosine, sine):
    half = heads.shape[-1] // 2
    first = heads[..., :half]
    second = heads[..., half:]
    across = cosine[:, None, :]
    along = sine[:, None, :]
    return jnp.concatenate(
        [first * across - second * along, second * across + first * along], axis=-1
    )


def unrotate(grad, cosine, sine):
    half = grad.shape[-1] // 2
    first = grad[..., :half]
    second = grad[..., half:]
    across = cosine[:, None, :]
    along = sine[:, None, :]
    return jnp.concatenate(
        [first * across + second * along, second * across - first * along], axis=-1
    )


def head_norm(heads, gain):
    scale = lax.rsqrt(jnp.mean(heads * heads, axis=-1, keepdims=True) + EPSILON)
    return (heads * scale * gain, scale)


def head_norm_back(heads, scale, gain, grad):
    weighted = grad * gain
    inner = jnp.mean(weighted * heads, axis=-1, keepdims=True)
    return scale * weighted - scale**3 * heads * inner


def probabilities(q_rot, keys, query_pos, key_pos):
    count, q_heads, width = q_rot.shape
    kv_heads = keys.shape[1]
    grouped = q_rot.reshape(count, kv_heads, q_heads // kv_heads, width)
    scores = (
        jnp.einsum("tkgd,lkd->kgtl", grouped, keys, preferred_element_type=jnp.float32)
        * SCORE_SCALE
    )
    gap = query_pos[:, None] - key_pos[None, :]
    allowed = (gap >= 0) & (gap < WINDOW_TOKENS) & (key_pos[None, :] >= 0)
    weights = jnp.where(allowed, jnp.exp(scores), 0.0)
    return (weights / jnp.sum(weights, axis=-1, keepdims=True), grouped)


def attention_forward(q_rot, keys, values, query_pos, key_pos):
    count, q_heads, width = q_rot.shape
    probability, grouped = probabilities(q_rot, keys, query_pos, key_pos)
    prob_low = probability.astype(jnp.bfloat16)
    mixed = jnp.einsum("kgtl,lkd->tkgd", prob_low, values, preferred_element_type=jnp.float32)
    return mixed.reshape(count, q_heads * width).astype(jnp.bfloat16)


def attention_backward(q_rot, keys, values, output_gradient, query_pos, key_pos):
    count, q_heads, width = q_rot.shape
    kv_heads = keys.shape[1]
    probability, grouped = probabilities(q_rot, keys, query_pos, key_pos)
    prob_low = probability.astype(jnp.bfloat16)
    grad_grouped = output_gradient.reshape(count, kv_heads, q_heads // kv_heads, width)
    grad_prob = jnp.einsum(
        "tkgd,lkd->kgtl", grad_grouped, values, preferred_element_type=jnp.float32
    )
    grad_values = jnp.einsum(
        "kgtl,tkgd->lkd", prob_low, grad_grouped, preferred_element_type=jnp.float32
    )
    inner = jnp.sum(probability * grad_prob, axis=-1, keepdims=True)
    grad_scores = (probability * (grad_prob - inner) * SCORE_SCALE).astype(jnp.bfloat16)
    grad_query = jnp.einsum(
        "kgtl,lkd->tkgd", grad_scores, keys, preferred_element_type=jnp.float32
    ).reshape(count, q_heads, width)
    grad_keys = jnp.einsum(
        "kgtl,tkgd->lkd", grad_scores, grouped, preferred_element_type=jnp.float32
    )
    return (grad_query, grad_keys, grad_values)


def on_device(
    tokens,
    out_grad,
    in_gain,
    query_gain,
    key_gain,
    post_gain,
    q_codes,
    q_scodes,
    q_second,
    kv_codes,
    kv_scodes,
    kv_second,
    o_codes,
    o_scodes,
    o_second,
    q_down,
    query_up,
    kv_down,
    key_value_up,
    output_down,
    output_up,
):
    count = tokens.shape[0]
    share = tokens.shape[1]
    ctx_rank = lax.axis_index("ctx")
    tp_rank = lax.axis_index("tp")
    column_start = tp_rank * share
    row_start = ctx_rank * q_codes.shape[0]
    q_width = query_up.shape[1]
    kv_width = key_value_up.shape[2]
    q_heads_here = q_width // HEAD_SIZE
    kv_heads_here = kv_width // HEAD_SIZE
    q_part = dequantize(q_codes, q_scodes, q_second, row_start)
    k_part = dequantize(kv_codes[0], kv_scodes[0], kv_second[0], row_start)
    v_part = dequantize(kv_codes[1], kv_scodes[1], kv_second[1], row_start)
    o_part = dequantize(o_codes, o_scodes, o_second, row_start)
    key_matrix, value_matrix = gather_pair(k_part, v_part, 1)
    q_part, o_part, key_matrix, value_matrix = lax.optimization_barrier(
        (q_part, o_part, key_matrix, value_matrix)
    )
    query_matrix, output_matrix = gather_pair(q_part, o_part, 2)
    whole_tokens = lax.all_gather(tokens, "tp", axis=1, tiled=True)
    wide = whole_tokens.astype(jnp.float32)
    row_scale = lax.rsqrt(jnp.mean(wide * wide, axis=1, keepdims=True) + EPSILON)
    normalized_input = (wide * row_scale * in_gain).astype(jnp.bfloat16)
    query_lowrank = jnp.dot(normalized_input, q_down, preferred_element_type=jnp.float32).astype(
        jnp.bfloat16
    )
    key_lowrank = jnp.dot(normalized_input, kv_down[0], preferred_element_type=jnp.float32).astype(
        jnp.bfloat16
    )
    value_lowrank = jnp.dot(
        normalized_input, kv_down[1], preferred_element_type=jnp.float32
    ).astype(jnp.bfloat16)
    query_rows = jnp.dot(
        normalized_input, query_matrix, preferred_element_type=jnp.float32
    ) + ADAPTER_SCALE * jnp.dot(query_lowrank, query_up, preferred_element_type=jnp.float32)
    key = jnp.dot(
        normalized_input, key_matrix, preferred_element_type=jnp.float32
    ) + ADAPTER_SCALE * jnp.dot(key_lowrank, key_value_up[0], preferred_element_type=jnp.float32)
    value_total = jnp.dot(
        normalized_input, value_matrix, preferred_element_type=jnp.float32
    ) + ADAPTER_SCALE * jnp.dot(value_lowrank, key_value_up[1], preferred_element_type=jnp.float32)
    value_rows = value_total.astype(jnp.bfloat16)
    query_pos = ctx_rank * count + jnp.arange(count, dtype=jnp.int32)
    key_pos = ctx_rank * count - WINDOW_TOKENS + jnp.arange(WINDOW_TOKENS + count, dtype=jnp.int32)
    cosine, sine = rope_tables(query_pos)
    q_heads = query_rows.reshape(count, q_heads_here, HEAD_SIZE)
    q_normed, q_scale = head_norm(q_heads, query_gain)
    q_rot = rotate(q_normed, cosine, sine).astype(jnp.bfloat16)
    key_head_rows = key.reshape(count, kv_heads_here, HEAD_SIZE)
    k_normed, k_scale = head_norm(key_head_rows, key_gain)
    k_rot = rotate(k_normed, cosine, sine).astype(jnp.bfloat16)
    piece_rows = min(WINDOW_TOKENS, count)
    pieces = WINDOW_TOKENS // piece_rows
    stacked = jnp.stack([k_rot.reshape(count, kv_width), value_rows])
    arrived = []
    for offset in range(pieces, 0, -1):
        arrived.append(from_behind(stacked, "ctx", offset))
    window = jnp.concatenate(arrived + [stacked], axis=1)
    window_keys = window[0].reshape(WINDOW_TOKENS + count, kv_heads_here, HEAD_SIZE)
    window_values = window[1].reshape(WINDOW_TOKENS + count, kv_heads_here, HEAD_SIZE)
    attended_rows = attention_forward(q_rot, window_keys, window_values, query_pos, key_pos)
    low_part = jnp.dot(attended_rows, output_down, preferred_element_type=jnp.float32)
    out_part = jnp.dot(attended_rows, output_matrix.T, preferred_element_type=jnp.float32)
    gain_mine = lax.dynamic_slice_in_dim(post_gain, column_start, share, 0)
    output_lowrank = lax.psum(low_part, "tp").astype(jnp.bfloat16)
    up_mine = lax.dynamic_slice_in_dim(output_up, column_start, share, 1)
    out_mine = lax.psum_scatter(
        out_part.astype(jnp.bfloat16), "tp", scatter_dimension=1, tiled=True
    ).astype(jnp.float32) + ADAPTER_SCALE * jnp.dot(output_lowrank, up_mine, preferred_element_type=jnp.float32)
    square_sum = lax.psum(jnp.sum(out_mine * out_mine, axis=1, keepdims=True), "tp")
    out_scale = lax.rsqrt(square_sum / D + EPSILON)
    mixed = (tokens.astype(jnp.float32) + out_mine * out_scale * gain_mine).astype(jnp.bfloat16)
    weighted_out = out_grad.astype(jnp.float32) * gain_mine
    out_inner = lax.psum(jnp.sum(weighted_out * out_mine, axis=1, keepdims=True), "tp") / D
    grad_mine = (out_scale * weighted_out - out_scale**3 * out_mine * out_inner).astype(
        jnp.bfloat16
    )
    output_gradient = lax.all_gather(grad_mine, "tp", axis=1, tiled=True)
    output_mixture = jnp.dot(
        output_gradient, output_up.T, preferred_element_type=jnp.float32
    ).astype(jnp.bfloat16)
    output_up_part = jnp.dot(output_lowrank.T, grad_mine, preferred_element_type=jnp.float32)
    output_down_part = jnp.dot(
        output_mixture.T, attended_rows, preferred_element_type=jnp.float32
    )
    attended_gradient = (
        jnp.dot(output_gradient, output_matrix, preferred_element_type=jnp.float32)
        + ADAPTER_SCALE * jnp.dot(output_mixture, output_down.T, preferred_element_type=jnp.float32)
    ).astype(jnp.bfloat16)
    query_grad, key_window_grad, value_window_grad = attention_backward(
        q_rot, window_keys, window_values, attended_gradient, query_pos, key_pos
    )
    window_grad = jnp.stack(
        [
            key_window_grad.reshape(WINDOW_TOKENS + count, kv_width),
            value_window_grad.reshape(WINDOW_TOKENS + count, kv_width),
        ]
    )
    front_rows = window_grad[:, :WINDOW_TOKENS].astype(jnp.bfloat16)
    own = window_grad[:, WINDOW_TOKENS:]
    returned = jnp.zeros((2, piece_rows, kv_width), jnp.float32)
    for offset in range(1, pieces + 1):
        piece = front_rows[:, (pieces - offset) * piece_rows : (pieces - offset + 1) * piece_rows]
        returned = returned + from_behind(piece, "ctx", -offset).astype(jnp.float32)
    own = jnp.concatenate([own[:, : count - piece_rows], own + returned], axis=1)
    q_norm_grad = unrotate(query_grad, cosine, sine)
    k_norm_grad = unrotate(own[0].reshape(count, kv_heads_here, HEAD_SIZE), cosine, sine)
    query_gradient_lowrank = (
        head_norm_back(q_heads, q_scale, query_gain, q_norm_grad)
        .reshape(count, q_width)
        .astype(jnp.bfloat16)
    )
    key_gradient_lowrank = (
        head_norm_back(key_head_rows, k_scale, key_gain, k_norm_grad)
        .reshape(count, kv_width)
        .astype(jnp.bfloat16)
    )
    value_gradient_lowrank = own[1].astype(jnp.bfloat16)
    query_mixture = jnp.dot(query_gradient_lowrank, query_up.T, preferred_element_type=jnp.float32)
    key_mixture = jnp.dot(
        key_gradient_lowrank, key_value_up[0].T, preferred_element_type=jnp.float32
    )
    value_mixture = jnp.dot(
        value_gradient_lowrank, key_value_up[1].T, preferred_element_type=jnp.float32
    )
    into_part = jnp.dot(query_gradient_lowrank, query_matrix.T, preferred_element_type=jnp.float32)
    into_part = into_part + jnp.dot(
        key_gradient_lowrank, key_matrix.T, preferred_element_type=jnp.float32
    )
    into_part = into_part + jnp.dot(
        value_gradient_lowrank, value_matrix.T, preferred_element_type=jnp.float32
    )
    query_mixture, key_mixture, value_mixture = lax.psum(
        (query_mixture, key_mixture, value_mixture), "tp"
    )
    query_mixture = query_mixture.astype(jnp.bfloat16)
    key_mixture = key_mixture.astype(jnp.bfloat16)
    value_mixture = value_mixture.astype(jnp.bfloat16)
    into_mine = lax.psum_scatter(
        into_part.astype(jnp.bfloat16), "tp", scatter_dimension=1, tiled=True
    ).astype(jnp.float32)
    q_down_mine = lax.dynamic_slice_in_dim(q_down, column_start, share, 0)
    k_down_mine = lax.dynamic_slice_in_dim(kv_down[0], column_start, share, 0)
    v_down_mine = lax.dynamic_slice_in_dim(kv_down[1], column_start, share, 0)
    adapter_term = (
        jnp.dot(query_mixture, q_down_mine.T, preferred_element_type=jnp.float32)
        + jnp.dot(key_mixture, k_down_mine.T, preferred_element_type=jnp.float32)
        + jnp.dot(value_mixture, v_down_mine.T, preferred_element_type=jnp.float32)
    )
    normalized_gradient = into_mine + ADAPTER_SCALE * adapter_term
    in_gain_mine = lax.dynamic_slice_in_dim(in_gain, column_start, share, 0)
    weighted_in = normalized_gradient * in_gain_mine
    wide_mine = tokens.astype(jnp.float32)
    in_inner = lax.psum(jnp.sum(weighted_in * wide_mine, axis=1, keepdims=True), "tp") / D
    tokens_grad = (
        out_grad.astype(jnp.float32) + row_scale * weighted_in - row_scale**3 * wide_mine * in_inner
    )
    in_projection = float(D) ** 0.5 * row_scale * in_inner
    normed_mine = (wide_mine * row_scale * in_gain_mine).astype(jnp.bfloat16)
    mixtures = jnp.concatenate([query_mixture, key_mixture, value_mixture], axis=1)
    down_part = jnp.concatenate(
        [jnp.dot(mixtures.T, normed_mine, preferred_element_type=jnp.float32), output_up_part]
    )
    up_part = jnp.concatenate(
        [
            jnp.dot(query_lowrank.T, query_gradient_lowrank, preferred_element_type=jnp.float32),
            jnp.dot(key_lowrank.T, key_gradient_lowrank, preferred_element_type=jnp.float32),
            jnp.dot(value_lowrank.T, value_gradient_lowrank, preferred_element_type=jnp.float32),
            output_down_part,
        ],
        axis=1,
    )
    down_sum, up_sum = reduce_gradients(ADAPTER_SCALE * down_part, ADAPTER_SCALE * up_part, 3)
    rank = query_up.shape[0]
    sharers = down_sum.shape[0]
    down_sum = down_sum.reshape(sharers, 4, rank, share)
    down_turned = down_sum[:, :3].transpose(1, 0, 3, 2).reshape(3, sharers * share, rank)
    query_down_gradient = down_turned[0]
    key_value_down_gradient = down_turned[1:]
    output_up_gradient = down_sum[:, 3].transpose(1, 0, 2).reshape(rank, sharers * share)
    query_up_gradient = up_sum[:, :q_width]
    key_value_up_gradient = jnp.stack(
        [
            up_sum[:, q_width : q_width + kv_width],
            up_sum[:, q_width + kv_width : q_width + 2 * kv_width],
        ]
    )
    output_down_gradient = up_sum[:, q_width + 2 * kv_width :].T
    return (
        mixed,
        tokens_grad,
        query_down_gradient,
        query_up_gradient,
        key_value_down_gradient,
        key_value_up_gradient,
        output_down_gradient,
        output_up_gradient,
        in_projection,
    )


def solution(mesh):
    placed = (
        P("ctx", "tp"),
        P("ctx", "tp"),
        P(),
        P(),
        P(),
        P(),
        P("ctx", "tp"),
        P("ctx", "tp"),
        P(None, "tp"),
        P(None, "ctx", "tp"),
        P(None, "ctx", "tp"),
        P(None, None, "tp"),
        P("ctx", "tp"),
        P("ctx", "tp"),
        P(None, "tp"),
        P(),
        P(None, "tp"),
        P(),
        P(None, None, "tp"),
        P("tp", None),
        P(),
    )
    return jax.shard_map(
        on_device,
        mesh=mesh,
        in_specs=placed,
        out_specs=(
            P("ctx", "tp"),
            P("ctx", "tp"),
            P(),
            P(None, "tp"),
            P(),
            P(None, None, "tp"),
            P("tp", None),
            P(),
            P("ctx", None),
        ),
        check_vma=False,
    )
```

```python
import functools

import jax
import jax.numpy as jnp
from jax import lax
from jax.experimental import pallas as pl
from jax.experimental.pallas import tpu as pltpu
from jax.sharding import PartitionSpec as P

D = 5376
HEAD_SIZE = 128
WINDOW_TOKENS = 1024
QBLOCK = 64
QGROUP = 256


NORMAL_FLOAT = (
    -1.0,
    -0.6961928009986877,
    -0.5250730514526367,
    -0.39491748809814453,
    -0.28444138169288635,
    -0.18477343022823334,
    -0.09105003625154495,
    0.0,
    0.07958029955625534,
    0.16093020141124725,
    0.24611230194568634,
    0.33791524171829224,
    0.44070982933044434,
    0.5626170039176941,
    0.7229568362236023,
    1.0,
)
EPSILON = 1e-06
ADAPTER_SCALE = 2.0
SCORE_SCALE = 168.0 ** (-0.5)
ROPE_BASE = 10000.0


def from_behind(shard, axis, by):
    devices = lax.axis_size(axis)
    pairs = [(i, i + by) for i in range(devices) if 0 <= i + by < devices]
    return lax.ppermute(shard, axis, pairs)


MESH = pl.DeviceIdType.MESH


def ring_place(index, devices):
    odd = index % 2
    return (1 - odd) * (index // 2) + odd * (devices - 1 - index // 2)


def ring_index(place, devices):
    back = place // (devices // 2)
    return (1 - back) * 2 * place + back * (2 * (devices - 1 - place) + 1)


def gather_kernel(devices, chunks, a_ref, b_ref, a_out, b_out, own_sem, send_sem, recv_sem):
    me = lax.axis_index("ctx")
    place = ring_place(me, devices)
    right = ring_index((place + 1) % devices, devices)
    left = ring_index((place + devices - 1) % devices, devices)
    barrier = pltpu.get_barrier_semaphore()
    for neighbour in (left, right):
        pl.semaphore_signal(barrier, inc=1, device_id={"ctx": neighbour}, device_id_type=MESH)
    pl.semaphore_wait(barrier, 2)
    own = []
    for way, (source, target) in enumerate(((a_ref, a_out), (b_ref, b_out))):
        own.append(pltpu.make_async_copy(source, target.at[me], own_sem.at[way]))
        own[-1].start()
    rows = a_ref.shape[0] // chunks
    copies = {}
    for step in range(devices - 1):
        for chunk in range(chunks):
            part = pl.ds(chunk * rows, rows)
            for way, (source, target) in enumerate(((a_ref, a_out), (b_ref, b_out))):
                if step > 0:
                    copies[step - 1, chunk, way].wait_recv()
                shift = devices - step if way == 0 else step
                owner = ring_index((place + shift) % devices, devices)
                copy = pltpu.make_async_remote_copy(
                    src_ref=source.at[part] if step == 0 else target.at[owner, part],
                    dst_ref=target.at[owner, part],
                    send_sem=send_sem.at[way, step * chunks + chunk],
                    recv_sem=recv_sem.at[way, step * chunks + chunk],
                    device_id={"ctx": right if way == 0 else left},
                    device_id_type=MESH,
                )
                copy.start()
                copies[step, chunk, way] = copy
    for chunk in range(chunks):
        for way in range(2):
            copies[devices - 2, chunk, way].wait_recv()
    for copy in copies.values():
        copy.wait_send()
    for copy in own:
        copy.wait()


def gather_pair(a, b, collective_id):
    devices = lax.axis_size("ctx")
    rows = a.shape[0]
    chunks = 3 if rows % 48 == 0 else 1
    count = (devices - 1) * chunks
    sent = (devices - 1) * (a.size + b.size) * 2
    gathered = pl.pallas_call(
        functools.partial(gather_kernel, devices, chunks),
        out_shape=[jax.ShapeDtypeStruct((devices,) + x.shape, x.dtype) for x in (a, b)],
        in_specs=[pl.BlockSpec(memory_space=pl.ANY)] * 2,
        out_specs=[pl.BlockSpec(memory_space=pl.ANY)] * 2,
        scratch_shapes=[
            pltpu.SemaphoreType.DMA((2,)),
            pltpu.SemaphoreType.DMA((2, count)),
            pltpu.SemaphoreType.DMA((2, count)),
        ],
        cost_estimate=pl.CostEstimate(flops=0, bytes_accessed=sent * 20, transcendentals=0),
        compiler_params=pltpu.CompilerParams(collective_id=collective_id, has_side_effects=True),
    )(a, b)
    return [x.reshape(devices * rows, x.shape[2]) for x in gathered]


def reduce_kernel(
    devices, sharers, split, g_ref, down_ref, up_ref, slots, summed, gathered, sems, side_sems
):
    me = lax.axis_index("ctx")
    side = lax.axis_index("tp")
    rows = g_ref.shape[0] // devices
    barrier = pltpu.get_barrier_semaphore()
    for k in range(1, devices):
        pl.semaphore_signal(
            barrier, inc=1, device_id={"ctx": (me + k) % devices}, device_id_type=MESH
        )
    for k in range(1, sharers):
        pl.semaphore_signal(
            barrier, inc=1, device_id={"tp": (side + k) % sharers}, device_id_type=MESH
        )
    pl.semaphore_wait(barrier, devices + sharers - 2)
    first = []
    for k in range(1, devices):
        other = (me + k) % devices
        copy = pltpu.make_async_remote_copy(
            src_ref=g_ref.at[pl.ds(pl.multiple_of(other * rows, rows), rows)],
            dst_ref=slots.at[k],
            send_sem=sems.at[0, k],
            recv_sem=sems.at[1, k],
            device_id={"ctx": other},
            device_id_type=MESH,
        )
        copy.start()
        first.append(copy)
    total = g_ref[pl.ds(pl.multiple_of(me * rows, rows), rows), :]
    for k in range(1, devices):
        first[k - 1].wait_recv()
        total = total + slots[k]
    summed[...] = total
    gathered[me] = total
    second = []
    for k in range(1, devices):
        copy = pltpu.make_async_remote_copy(
            src_ref=summed,
            dst_ref=gathered.at[me],
            send_sem=sems.at[2, k],
            recv_sem=sems.at[3, k],
            device_id={"ctx": (me + k) % devices},
            device_id_type=MESH,
        )
        copy.start()
        second.append(copy)
    for copy in second:
        copy.wait_recv()
    third = []
    for k in range(1, sharers):
        copy = pltpu.make_async_remote_copy(
            src_ref=gathered.at[:, :, pl.ds(0, split)],
            dst_ref=down_ref.at[side],
            send_sem=side_sems.at[0, k],
            recv_sem=side_sems.at[1, k],
            device_id={"tp": (side + k) % sharers},
            device_id_type=MESH,
        )
        copy.start()
        third.append(copy)
    down_ref[side] = gathered[:, :, :split]
    up_ref[...] = gathered[:, :, split:]
    for copy in first + second:
        copy.wait_send()
    for copy in third:
        copy.wait()


def reduce_gradients(down, up, collective_id):
    devices = lax.axis_size("ctx")
    sharers = lax.axis_size("tp")
    height, width = down.shape
    up_shape = up.shape
    if height % (8 * devices) or up.size % (128 * height):
        down, up = lax.psum((down, up), "ctx")
        return lax.all_gather(down, "tp"), up
    up = up.reshape(height, up.size // height)
    split = -(-width // 128) * 128
    packed = jnp.concatenate([down, jnp.zeros((height, split - width), jnp.float32), up], axis=1)
    rows = height // devices
    whole = packed.shape[1]
    down, up = pl.pallas_call(
        functools.partial(reduce_kernel, devices, sharers, split),
        out_shape=[
            jax.ShapeDtypeStruct((sharers, devices, rows, split), jnp.float32),
            jax.ShapeDtypeStruct((devices, rows, whole - split), jnp.float32),
        ],
        in_specs=[pl.BlockSpec(memory_space=pltpu.VMEM)],
        out_specs=[pl.BlockSpec(memory_space=pltpu.VMEM)] * 2,
        scratch_shapes=[
            pltpu.VMEM((devices, rows, whole), jnp.float32),
            pltpu.VMEM((rows, whole), jnp.float32),
            pltpu.VMEM((devices, rows, whole), jnp.float32),
            pltpu.SemaphoreType.DMA((4, devices)),
            pltpu.SemaphoreType.DMA((2, sharers)),
        ],
        compiler_params=pltpu.CompilerParams(collective_id=collective_id, has_side_effects=True),
    )(packed)
    return down.reshape(sharers, height, split)[:, :, :width], up.reshape(up_shape)


def share_kernel(chunks, parts_ref, small_ref, out_ref, small_out, *scratch):
    core_in, staged, cross_in, small_in, core_sems, cross_sems, small_sems = scratch
    side = lax.axis_index("tp")
    chip, core = side // 2, side % 2
    partner = chip * 2 + 1 - core
    across = (1 - chip) * 2 + core
    barrier = pltpu.get_barrier_semaphore()
    for k in range(1, 4):
        pl.semaphore_signal(barrier, inc=1, device_id={"tp": (side + k) % 4}, device_id_type=MESH)
    pl.semaphore_wait(barrier, 3)
    rows = parts_ref.shape[1] // chunks

    def core_copy(far, chunk):
        chip_to = far * (1 - chip) + (1 - far) * chip
        part = pl.ds(chunk * rows, rows)
        return pltpu.make_async_remote_copy(
            src_ref=parts_ref.at[chip_to * 2 + 1 - core, part],
            dst_ref=core_in.at[far, part],
            send_sem=core_sems.at[0, far, chunk],
            recv_sem=core_sems.at[1, far, chunk],
            device_id={"tp": partner},
            device_id_type=MESH,
        )

    to_core = {}
    for far in (1, 0):
        for chunk in range(chunks):
            to_core[far, chunk] = core_copy(far, chunk)
            to_core[far, chunk].start()
    to_all = []
    for k in range(1, 4):
        copy = pltpu.make_async_remote_copy(
            src_ref=small_ref,
            dst_ref=small_in.at[side],
            send_sem=small_sems.at[0, k],
            recv_sem=small_sems.at[1, k],
            device_id={"tp": (side + k) % 4},
            device_id_type=MESH,
        )
        copy.start()
        to_all.append(copy)
    small_in[side] = small_ref[...]
    to_across = []
    for chunk in range(chunks):
        part = pl.ds(chunk * rows, rows)
        to_core[1, chunk].wait_recv()
        staged[part, :] = (
            parts_ref[across, part, :].astype(jnp.float32)
            + core_in[1, part, :].astype(jnp.float32)
        ).astype(jnp.bfloat16)
        copy = pltpu.make_async_remote_copy(
            src_ref=staged.at[part],
            dst_ref=cross_in.at[part],
            send_sem=cross_sems.at[0, chunk],
            recv_sem=cross_sems.at[1, chunk],
            device_id={"tp": across},
            device_id_type=MESH,
        )
        copy.start()
        to_across.append(copy)
    for chunk in range(chunks):
        part = pl.ds(chunk * rows, rows)
        to_core[0, chunk].wait_recv()
        out_ref[part, :] = parts_ref[side, part, :].astype(jnp.float32) + core_in[
            0, part, :
        ].astype(jnp.float32)
    for copy in to_all:
        copy.wait_recv()
    small_out[...] = (small_in[0] + small_in[1]) + (small_in[2] + small_in[3])
    for chunk in range(chunks):
        part = pl.ds(chunk * rows, rows)
        to_across[chunk].wait_recv()
        out_ref[part, :] = out_ref[part, :] + cross_in[part, :].astype(jnp.float32)
    for copy in list(to_core.values()) + to_all + to_across:
        copy.wait_send()


def share_sums(parts, small, collective_id):
    sharers = lax.axis_size("tp")
    _, count, share = parts.shape
    if sharers != 4 or count % 64:
        mine = lax.psum_scatter(parts, "tp", scatter_dimension=0, tiled=False)
        return mine.astype(jnp.float32), lax.psum(small, "tp")
    width = small.shape[1]
    lanes = -(-width // 128) * 128
    small = jnp.pad(small, ((0, 0), (0, lanes - width)))
    chunks = 4
    mine, small = pl.pallas_call(
        functools.partial(share_kernel, chunks),
        out_shape=[
            jax.ShapeDtypeStruct((count, share), jnp.float32),
            jax.ShapeDtypeStruct((count, lanes), jnp.float32),
        ],
        in_specs=[pl.BlockSpec(memory_space=pltpu.VMEM)] * 2,
        out_specs=[pl.BlockSpec(memory_space=pltpu.VMEM)] * 2,
        scratch_shapes=[
            pltpu.VMEM((2, count, share), jnp.bfloat16),
            pltpu.VMEM((count, share), jnp.bfloat16),
            pltpu.VMEM((count, share), jnp.bfloat16),
            pltpu.VMEM((sharers, count, lanes), jnp.float32),
            pltpu.SemaphoreType.DMA((2, 2, chunks)),
            pltpu.SemaphoreType.DMA((2, chunks)),
            pltpu.SemaphoreType.DMA((2, sharers)),
        ],
        compiler_params=pltpu.CompilerParams(collective_id=collective_id, has_side_effects=True),
    )(parts, small)
    return mine, small[:, :width]


def dequantize(codes, scodes, second, row_start):
    height, width = codes.shape
    levels = jnp.zeros(codes.shape, jnp.float32)
    for level in range(16):
        levels = jnp.where(codes == level, jnp.float32(NORMAL_FLOAT[level]), levels)
    group_ids = (row_start + jnp.arange(height, dtype=jnp.int32)) // QGROUP
    group_list = jnp.arange(second.shape[0], dtype=jnp.int32)
    picker = (group_ids[:, None] == group_list[None, :]).astype(jnp.float32)
    second_rows = jnp.dot(picker, second, precision=lax.Precision.HIGHEST)
    absmax = second_rows * ((scodes.astype(jnp.float32) + 1.0) / 256.0)
    scaled = levels.reshape(height, width // QBLOCK, QBLOCK) * absmax[:, :, None]
    return scaled.reshape(height, width).astype(jnp.bfloat16)


def rope_tables(positions):
    half = HEAD_SIZE // 2
    exponent = jnp.arange(half, dtype=jnp.float32) * (2.0 / HEAD_SIZE)
    frequency = jnp.power(jnp.float32(ROPE_BASE), -exponent)
    angle = positions.astype(jnp.float32)[:, None] * frequency[None, :]
    return (jnp.cos(angle), jnp.sin(angle))


def rotate(heads, cosine, sine):
    half = heads.shape[-1] // 2
    first = heads[..., :half]
    second = heads[..., half:]
    across = cosine[:, None, :]
    along = sine[:, None, :]
    return jnp.concatenate(
        [first * across - second * along, second * across + first * along], axis=-1
    )


def unrotate(grad, cosine, sine):
    half = grad.shape[-1] // 2
    first = grad[..., :half]
    second = grad[..., half:]
    across = cosine[:, None, :]
    along = sine[:, None, :]
    return jnp.concatenate(
        [first * across + second * along, second * across - first * along], axis=-1
    )


def head_norm(heads, gain):
    scale = lax.rsqrt(jnp.mean(heads * heads, axis=-1, keepdims=True) + EPSILON)
    return (heads * scale * gain, scale)


def head_norm_back(heads, scale, gain, grad):
    weighted = grad * gain
    inner = jnp.mean(weighted * heads, axis=-1, keepdims=True)
    return scale * weighted - scale**3 * heads * inner


def probabilities(q_rot, keys, query_pos, key_pos):
    count, q_heads, width = q_rot.shape
    kv_heads = keys.shape[1]
    grouped = q_rot.reshape(count, kv_heads, q_heads // kv_heads, width)
    scores = (
        jnp.einsum("tkgd,lkd->kgtl", grouped, keys, preferred_element_type=jnp.float32)
        * SCORE_SCALE
    )
    gap = query_pos[:, None] - key_pos[None, :]
    allowed = (gap >= 0) & (gap < WINDOW_TOKENS) & (key_pos[None, :] >= 0)
    weights = jnp.where(allowed, jnp.exp(scores), 0.0)
    return (weights / jnp.sum(weights, axis=-1, keepdims=True), grouped)


def attention_forward(q_rot, keys, values, query_pos, key_pos):
    count, q_heads, width = q_rot.shape
    probability, grouped = probabilities(q_rot, keys, query_pos, key_pos)
    prob_low = probability.astype(jnp.bfloat16)
    mixed = jnp.einsum("kgtl,lkd->tkgd", prob_low, values, preferred_element_type=jnp.float32)
    return mixed.reshape(count, q_heads * width).astype(jnp.bfloat16)


def attention_backward(q_rot, keys, values, output_gradient, query_pos, key_pos):
    count, q_heads, width = q_rot.shape
    kv_heads = keys.shape[1]
    probability, grouped = probabilities(q_rot, keys, query_pos, key_pos)
    prob_low = probability.astype(jnp.bfloat16)
    grad_grouped = output_gradient.reshape(count, kv_heads, q_heads // kv_heads, width)
    grad_prob = jnp.einsum(
        "tkgd,lkd->kgtl", grad_grouped, values, preferred_element_type=jnp.float32
    )
    grad_values = jnp.einsum(
        "kgtl,tkgd->lkd", prob_low, grad_grouped, preferred_element_type=jnp.float32
    )
    inner = jnp.sum(probability * grad_prob, axis=-1, keepdims=True)
    grad_scores = (probability * (grad_prob - inner) * SCORE_SCALE).astype(jnp.bfloat16)
    grad_query = jnp.einsum(
        "kgtl,lkd->tkgd", grad_scores, keys, preferred_element_type=jnp.float32
    ).reshape(count, q_heads, width)
    grad_keys = jnp.einsum(
        "kgtl,tkgd->lkd", grad_scores, grouped, preferred_element_type=jnp.float32
    )
    return (grad_query, grad_keys, grad_values)


def on_device(
    tokens,
    out_grad,
    in_gain,
    query_gain,
    key_gain,
    post_gain,
    q_codes,
    q_scodes,
    q_second,
    kv_codes,
    kv_scodes,
    kv_second,
    o_codes,
    o_scodes,
    o_second,
    q_down,
    query_up,
    kv_down,
    key_value_up,
    output_down,
    output_up,
):
    count = tokens.shape[0]
    share = tokens.shape[1]
    ctx_rank = lax.axis_index("ctx")
    tp_rank = lax.axis_index("tp")
    column_start = tp_rank * share
    row_start = ctx_rank * q_codes.shape[0]
    q_width = query_up.shape[1]
    kv_width = key_value_up.shape[2]
    q_heads_here = q_width // HEAD_SIZE
    kv_heads_here = kv_width // HEAD_SIZE
    q_part = dequantize(q_codes, q_scodes, q_second, row_start)
    k_part = dequantize(kv_codes[0], kv_scodes[0], kv_second[0], row_start)
    v_part = dequantize(kv_codes[1], kv_scodes[1], kv_second[1], row_start)
    o_part = dequantize(o_codes, o_scodes, o_second, row_start)
    key_matrix, value_matrix = gather_pair(k_part, v_part, 1)
    whole_tokens = lax.all_gather(tokens, "tp", axis=1, tiled=True)
    wide = whole_tokens.astype(jnp.float32)
    row_scale = lax.rsqrt(jnp.mean(wide * wide, axis=1, keepdims=True) + EPSILON)
    normalized_input = (wide * row_scale * in_gain).astype(jnp.bfloat16)
    query_lowrank = jnp.dot(normalized_input, q_down, preferred_element_type=jnp.float32).astype(
        jnp.bfloat16
    )
    key_lowrank = jnp.dot(normalized_input, kv_down[0], preferred_element_type=jnp.float32).astype(
        jnp.bfloat16
    )
    value_lowrank = jnp.dot(
        normalized_input, kv_down[1], preferred_element_type=jnp.float32
    ).astype(jnp.bfloat16)
    key = jnp.dot(
        normalized_input, key_matrix, preferred_element_type=jnp.float32
    ) + ADAPTER_SCALE * jnp.dot(key_lowrank, key_value_up[0], preferred_element_type=jnp.float32)
    value_total = jnp.dot(
        normalized_input, value_matrix, preferred_element_type=jnp.float32
    ) + ADAPTER_SCALE * jnp.dot(value_lowrank, key_value_up[1], preferred_element_type=jnp.float32)
    value_rows = value_total.astype(jnp.bfloat16)
    query_pos = ctx_rank * count + jnp.arange(count, dtype=jnp.int32)
    key_pos = ctx_rank * count - WINDOW_TOKENS + jnp.arange(WINDOW_TOKENS + count, dtype=jnp.int32)
    cosine, sine = rope_tables(query_pos)
    key_head_rows = key.reshape(count, kv_heads_here, HEAD_SIZE)
    k_normed, k_scale = head_norm(key_head_rows, key_gain)
    k_rot = rotate(k_normed, cosine, sine).astype(jnp.bfloat16)
    piece_rows = min(WINDOW_TOKENS, count)
    pieces = WINDOW_TOKENS // piece_rows
    stacked = jnp.stack([k_rot.reshape(count, kv_width), value_rows])
    q_part, o_part, stacked = lax.optimization_barrier((q_part, o_part, stacked))
    arrived = []
    for offset in range(pieces, 0, -1):
        arrived.append(from_behind(stacked, "ctx", offset))
    query_matrix, output_matrix = gather_pair(q_part, o_part, 2)
    query_rows = jnp.dot(
        normalized_input, query_matrix, preferred_element_type=jnp.float32
    ) + ADAPTER_SCALE * jnp.dot(query_lowrank, query_up, preferred_element_type=jnp.float32)
    q_heads = query_rows.reshape(count, q_heads_here, HEAD_SIZE)
    q_normed, q_scale = head_norm(q_heads, query_gain)
    q_rot = rotate(q_normed, cosine, sine).astype(jnp.bfloat16)
    window = jnp.concatenate(arrived + [stacked], axis=1)
    window_keys = window[0].reshape(WINDOW_TOKENS + count, kv_heads_here, HEAD_SIZE)
    window_values = window[1].reshape(WINDOW_TOKENS + count, kv_heads_here, HEAD_SIZE)
    attended_rows = attention_forward(q_rot, window_keys, window_values, query_pos, key_pos)
    low_part = jnp.dot(attended_rows, output_down, preferred_element_type=jnp.float32)
    sharers = lax.axis_size("tp")
    out_part = jnp.stack(
        [
            jnp.dot(
                attended_rows,
                output_matrix[k * share : (k + 1) * share].T,
                preferred_element_type=jnp.float32,
            ).astype(jnp.bfloat16)
            for k in range(sharers)
        ]
    )
    out_mine, low_sum = share_sums(out_part, low_part, 4)
    gain_mine = lax.dynamic_slice_in_dim(post_gain, column_start, share, 0)
    output_lowrank = low_sum.astype(jnp.bfloat16)
    up_mine = lax.dynamic_slice_in_dim(output_up, column_start, share, 1)
    out_mine = out_mine + ADAPTER_SCALE * jnp.dot(output_lowrank, up_mine, preferred_element_type=jnp.float32)
    square_sum = lax.psum(jnp.sum(out_mine * out_mine, axis=1, keepdims=True), "tp")
    out_scale = lax.rsqrt(square_sum / D + EPSILON)
    mixed = (tokens.astype(jnp.float32) + out_mine * out_scale * gain_mine).astype(jnp.bfloat16)
    weighted_out = out_grad.astype(jnp.float32) * gain_mine
    out_inner = lax.psum(jnp.sum(weighted_out * out_mine, axis=1, keepdims=True), "tp") / D
    grad_mine = (out_scale * weighted_out - out_scale**3 * out_mine * out_inner).astype(
        jnp.bfloat16
    )
    output_gradient = lax.all_gather(grad_mine, "tp", axis=1, tiled=True)
    output_mixture = jnp.dot(
        output_gradient, output_up.T, preferred_element_type=jnp.float32
    ).astype(jnp.bfloat16)
    output_up_part = jnp.dot(output_lowrank.T, grad_mine, preferred_element_type=jnp.float32)
    output_down_part = jnp.dot(
        output_mixture.T, attended_rows, preferred_element_type=jnp.float32
    )
    attended_gradient = (
        jnp.dot(output_gradient, output_matrix, preferred_element_type=jnp.float32)
        + ADAPTER_SCALE * jnp.dot(output_mixture, output_down.T, preferred_element_type=jnp.float32)
    ).astype(jnp.bfloat16)
    query_grad, key_window_grad, value_window_grad = attention_backward(
        q_rot, window_keys, window_values, attended_gradient, query_pos, key_pos
    )
    window_grad = jnp.stack(
        [
            key_window_grad.reshape(WINDOW_TOKENS + count, kv_width),
            value_window_grad.reshape(WINDOW_TOKENS + count, kv_width),
        ]
    )
    front_rows = window_grad[:, :WINDOW_TOKENS].astype(jnp.bfloat16)
    own = window_grad[:, WINDOW_TOKENS:]
    returned = jnp.zeros((2, piece_rows, kv_width), jnp.float32)
    for offset in range(1, pieces + 1):
        piece = front_rows[:, (pieces - offset) * piece_rows : (pieces - offset + 1) * piece_rows]
        returned = returned + from_behind(piece, "ctx", -offset).astype(jnp.float32)
    own = jnp.concatenate([own[:, : count - piece_rows], own + returned], axis=1)
    q_norm_grad = unrotate(query_grad, cosine, sine)
    k_norm_grad = unrotate(own[0].reshape(count, kv_heads_here, HEAD_SIZE), cosine, sine)
    query_gradient_lowrank = (
        head_norm_back(q_heads, q_scale, query_gain, q_norm_grad)
        .reshape(count, q_width)
        .astype(jnp.bfloat16)
    )
    key_gradient_lowrank = (
        head_norm_back(key_head_rows, k_scale, key_gain, k_norm_grad)
        .reshape(count, kv_width)
        .astype(jnp.bfloat16)
    )
    value_gradient_lowrank = own[1].astype(jnp.bfloat16)
    query_mixture = jnp.dot(query_gradient_lowrank, query_up.T, preferred_element_type=jnp.float32)
    key_mixture = jnp.dot(
        key_gradient_lowrank, key_value_up[0].T, preferred_element_type=jnp.float32
    )
    value_mixture = jnp.dot(
        value_gradient_lowrank, key_value_up[1].T, preferred_element_type=jnp.float32
    )
    into_parts = []
    for k in range(sharers):
        rows = slice(k * share, (k + 1) * share)
        into_part = jnp.dot(
            query_gradient_lowrank, query_matrix[rows].T, preferred_element_type=jnp.float32
        )
        into_part = into_part + jnp.dot(
            key_gradient_lowrank, key_matrix[rows].T, preferred_element_type=jnp.float32
        )
        into_part = into_part + jnp.dot(
            value_gradient_lowrank, value_matrix[rows].T, preferred_element_type=jnp.float32
        )
        into_parts.append(into_part.astype(jnp.bfloat16))
    into_mine, mixture_sum = share_sums(
        jnp.stack(into_parts),
        jnp.concatenate([query_mixture, key_mixture, value_mixture], axis=1),
        5,
    )
    query_mixture, key_mixture, value_mixture = jnp.split(mixture_sum, 3, axis=1)
    query_mixture = query_mixture.astype(jnp.bfloat16)
    key_mixture = key_mixture.astype(jnp.bfloat16)
    value_mixture = value_mixture.astype(jnp.bfloat16)
    q_down_mine = lax.dynamic_slice_in_dim(q_down, column_start, share, 0)
    k_down_mine = lax.dynamic_slice_in_dim(kv_down[0], column_start, share, 0)
    v_down_mine = lax.dynamic_slice_in_dim(kv_down[1], column_start, share, 0)
    adapter_term = (
        jnp.dot(query_mixture, q_down_mine.T, preferred_element_type=jnp.float32)
        + jnp.dot(key_mixture, k_down_mine.T, preferred_element_type=jnp.float32)
        + jnp.dot(value_mixture, v_down_mine.T, preferred_element_type=jnp.float32)
    )
    normalized_gradient = into_mine + ADAPTER_SCALE * adapter_term
    in_gain_mine = lax.dynamic_slice_in_dim(in_gain, column_start, share, 0)
    weighted_in = normalized_gradient * in_gain_mine
    wide_mine = tokens.astype(jnp.float32)
    in_inner = lax.psum(jnp.sum(weighted_in * wide_mine, axis=1, keepdims=True), "tp") / D
    tokens_grad = (
        out_grad.astype(jnp.float32) + row_scale * weighted_in - row_scale**3 * wide_mine * in_inner
    )
    in_projection = float(D) ** 0.5 * row_scale * in_inner
    normed_mine = (wide_mine * row_scale * in_gain_mine).astype(jnp.bfloat16)
    mixtures = jnp.concatenate([query_mixture, key_mixture, value_mixture], axis=1)
    down_part = jnp.concatenate(
        [jnp.dot(mixtures.T, normed_mine, preferred_element_type=jnp.float32), output_up_part]
    )
    up_part = jnp.concatenate(
        [
            jnp.dot(query_lowrank.T, query_gradient_lowrank, preferred_element_type=jnp.float32),
            jnp.dot(key_lowrank.T, key_gradient_lowrank, preferred_element_type=jnp.float32),
            jnp.dot(value_lowrank.T, value_gradient_lowrank, preferred_element_type=jnp.float32),
            output_down_part,
        ],
        axis=1,
    )
    down_sum, up_sum = reduce_gradients(ADAPTER_SCALE * down_part, ADAPTER_SCALE * up_part, 3)
    rank = query_up.shape[0]
    down_sum = down_sum.reshape(sharers, 4, rank, share)
    down_turned = down_sum[:, :3].transpose(1, 0, 3, 2).reshape(3, sharers * share, rank)
    query_down_gradient = down_turned[0]
    key_value_down_gradient = down_turned[1:]
    output_up_gradient = down_sum[:, 3].transpose(1, 0, 2).reshape(rank, sharers * share)
    query_up_gradient = up_sum[:, :q_width]
    key_value_up_gradient = jnp.stack(
        [
            up_sum[:, q_width : q_width + kv_width],
            up_sum[:, q_width + kv_width : q_width + 2 * kv_width],
        ]
    )
    output_down_gradient = up_sum[:, q_width + 2 * kv_width :].T
    return (
        mixed,
        tokens_grad,
        query_down_gradient,
        query_up_gradient,
        key_value_down_gradient,
        key_value_up_gradient,
        output_down_gradient,
        output_up_gradient,
        in_projection,
    )


def solution(mesh):
    placed = (
        P("ctx", "tp"),
        P("ctx", "tp"),
        P(),
        P(),
        P(),
        P(),
        P("ctx", "tp"),
        P("ctx", "tp"),
        P(None, "tp"),
        P(None, "ctx", "tp"),
        P(None, "ctx", "tp"),
        P(None, None, "tp"),
        P("ctx", "tp"),
        P("ctx", "tp"),
        P(None, "tp"),
        P(),
        P(None, "tp"),
        P(),
        P(None, None, "tp"),
        P("tp", None),
        P(),
    )
    return jax.shard_map(
        on_device,
        mesh=mesh,
        in_specs=placed,
        out_specs=(
            P("ctx", "tp"),
            P("ctx", "tp"),
            P(),
            P(None, "tp"),
            P(),
            P(None, None, "tp"),
            P("tp", None),
            P(),
            P("ctx", None),
        ),
        check_vma=False,
    )
```

```python
import functools

import jax
import jax.numpy as jnp
from jax import lax
from jax.experimental import pallas as pl
from jax.experimental.pallas import tpu as pltpu
from jax.sharding import PartitionSpec as P

D = 5376
HEAD_SIZE = 128
WINDOW_TOKENS = 1024
QBLOCK = 64
QGROUP = 256


NORMAL_FLOAT = (
    -1.0,
    -0.6961928009986877,
    -0.5250730514526367,
    -0.39491748809814453,
    -0.28444138169288635,
    -0.18477343022823334,
    -0.09105003625154495,
    0.0,
    0.07958029955625534,
    0.16093020141124725,
    0.24611230194568634,
    0.33791524171829224,
    0.44070982933044434,
    0.5626170039176941,
    0.7229568362236023,
    1.0,
)
EPSILON = 1e-06
ADAPTER_SCALE = 2.0
SCORE_SCALE = 168.0 ** (-0.5)
ROPE_BASE = 10000.0


def from_behind(shard, axis, by):
    devices = lax.axis_size(axis)
    pairs = [(i, i + by) for i in range(devices) if 0 <= i + by < devices]
    return lax.ppermute(shard, axis, pairs)


MESH = pl.DeviceIdType.MESH


def ring_place(index, devices):
    odd = index % 2
    return (1 - odd) * (index // 2) + odd * (devices - 1 - index // 2)


def ring_index(place, devices):
    back = place // (devices // 2)
    return (1 - back) * 2 * place + back * (2 * (devices - 1 - place) + 1)


def gather_kernel(devices, chunks, a_ref, b_ref, a_out, b_out, own_sem, send_sem, recv_sem):
    me = lax.axis_index("ctx")
    place = ring_place(me, devices)
    right = ring_index((place + 1) % devices, devices)
    left = ring_index((place + devices - 1) % devices, devices)
    barrier = pltpu.get_barrier_semaphore()
    for neighbour in (left, right):
        pl.semaphore_signal(barrier, inc=1, device_id={"ctx": neighbour}, device_id_type=MESH)
    pl.semaphore_wait(barrier, 2)
    own = []
    for way, (source, target) in enumerate(((a_ref, a_out), (b_ref, b_out))):
        own.append(pltpu.make_async_copy(source, target.at[me], own_sem.at[way]))
        own[-1].start()
    rows = a_ref.shape[0] // chunks
    copies = {}
    for step in range(devices - 1):
        for chunk in range(chunks):
            part = pl.ds(chunk * rows, rows)
            for way, (source, target) in enumerate(((a_ref, a_out), (b_ref, b_out))):
                if step > 0:
                    copies[step - 1, chunk, way].wait_recv()
                shift = devices - step if way == 0 else step
                owner = ring_index((place + shift) % devices, devices)
                copy = pltpu.make_async_remote_copy(
                    src_ref=source.at[part] if step == 0 else target.at[owner, part],
                    dst_ref=target.at[owner, part],
                    send_sem=send_sem.at[way, step * chunks + chunk],
                    recv_sem=recv_sem.at[way, step * chunks + chunk],
                    device_id={"ctx": right if way == 0 else left},
                    device_id_type=MESH,
                )
                copy.start()
                copies[step, chunk, way] = copy
    for chunk in range(chunks):
        for way in range(2):
            copies[devices - 2, chunk, way].wait_recv()
    for copy in copies.values():
        copy.wait_send()
    for copy in own:
        copy.wait()


def gather_pair(a, b, collective_id):
    devices = lax.axis_size("ctx")
    rows = a.shape[0]
    chunks = 3 if rows % 48 == 0 else 1
    count = (devices - 1) * chunks
    sent = (devices - 1) * (a.size + b.size) * 2
    gathered = pl.pallas_call(
        functools.partial(gather_kernel, devices, chunks),
        out_shape=[jax.ShapeDtypeStruct((devices,) + x.shape, x.dtype) for x in (a, b)],
        in_specs=[pl.BlockSpec(memory_space=pl.ANY)] * 2,
        out_specs=[pl.BlockSpec(memory_space=pl.ANY)] * 2,
        scratch_shapes=[
            pltpu.SemaphoreType.DMA((2,)),
            pltpu.SemaphoreType.DMA((2, count)),
            pltpu.SemaphoreType.DMA((2, count)),
        ],
        cost_estimate=pl.CostEstimate(flops=0, bytes_accessed=sent * 20, transcendentals=0),
        compiler_params=pltpu.CompilerParams(collective_id=collective_id, has_side_effects=True),
    )(a, b)
    return [x.reshape(devices * rows, x.shape[2]) for x in gathered]


def reduce_kernel(
    devices, sharers, split, g_ref, down_ref, up_ref, slots, summed, gathered, sems, side_sems
):
    me = lax.axis_index("ctx")
    side = lax.axis_index("tp")
    rows = g_ref.shape[0] // devices
    barrier = pltpu.get_barrier_semaphore()
    for k in range(1, devices):
        pl.semaphore_signal(
            barrier, inc=1, device_id={"ctx": (me + k) % devices}, device_id_type=MESH
        )
    for k in range(1, sharers):
        pl.semaphore_signal(
            barrier, inc=1, device_id={"tp": (side + k) % sharers}, device_id_type=MESH
        )
    pl.semaphore_wait(barrier, devices + sharers - 2)
    first = []
    for k in range(1, devices):
        other = (me + k) % devices
        copy = pltpu.make_async_remote_copy(
            src_ref=g_ref.at[pl.ds(pl.multiple_of(other * rows, rows), rows)],
            dst_ref=slots.at[k],
            send_sem=sems.at[0, k],
            recv_sem=sems.at[1, k],
            device_id={"ctx": other},
            device_id_type=MESH,
        )
        copy.start()
        first.append(copy)
    total = g_ref[pl.ds(pl.multiple_of(me * rows, rows), rows), :]
    for k in range(1, devices):
        first[k - 1].wait_recv()
        total = total + slots[k]
    summed[...] = total
    gathered[me] = total
    second = []
    for k in range(1, devices):
        copy = pltpu.make_async_remote_copy(
            src_ref=summed,
            dst_ref=gathered.at[me],
            send_sem=sems.at[2, k],
            recv_sem=sems.at[3, k],
            device_id={"ctx": (me + k) % devices},
            device_id_type=MESH,
        )
        copy.start()
        second.append(copy)
    for copy in second:
        copy.wait_recv()
    third = []
    for k in range(1, sharers):
        copy = pltpu.make_async_remote_copy(
            src_ref=gathered.at[:, :, pl.ds(0, split)],
            dst_ref=down_ref.at[side],
            send_sem=side_sems.at[0, k],
            recv_sem=side_sems.at[1, k],
            device_id={"tp": (side + k) % sharers},
            device_id_type=MESH,
        )
        copy.start()
        third.append(copy)
    down_ref[side] = gathered[:, :, :split]
    up_ref[...] = gathered[:, :, split:]
    for copy in first + second:
        copy.wait_send()
    for copy in third:
        copy.wait()


def reduce_gradients(down, up, collective_id):
    devices = lax.axis_size("ctx")
    sharers = lax.axis_size("tp")
    height, width = down.shape
    up_shape = up.shape
    if height % (8 * devices) or up.size % (128 * height):
        down, up = lax.psum((down, up), "ctx")
        return lax.all_gather(down, "tp"), up
    up = up.reshape(height, up.size // height)
    split = -(-width // 128) * 128
    packed = jnp.concatenate([down, jnp.zeros((height, split - width), jnp.float32), up], axis=1)
    rows = height // devices
    whole = packed.shape[1]
    down, up = pl.pallas_call(
        functools.partial(reduce_kernel, devices, sharers, split),
        out_shape=[
            jax.ShapeDtypeStruct((sharers, devices, rows, split), jnp.float32),
            jax.ShapeDtypeStruct((devices, rows, whole - split), jnp.float32),
        ],
        in_specs=[pl.BlockSpec(memory_space=pltpu.VMEM)],
        out_specs=[pl.BlockSpec(memory_space=pltpu.VMEM)] * 2,
        scratch_shapes=[
            pltpu.VMEM((devices, rows, whole), jnp.float32),
            pltpu.VMEM((rows, whole), jnp.float32),
            pltpu.VMEM((devices, rows, whole), jnp.float32),
            pltpu.SemaphoreType.DMA((4, devices)),
            pltpu.SemaphoreType.DMA((2, sharers)),
        ],
        compiler_params=pltpu.CompilerParams(collective_id=collective_id, has_side_effects=True),
    )(packed)
    return down.reshape(sharers, height, split)[:, :, :width], up.reshape(up_shape)


def share_kernel(chunks, parts_ref, small_ref, out_ref, small_out, *scratch):
    core_in, staged, cross_in, small_in, core_sems, cross_sems, small_sems = scratch
    side = lax.axis_index("tp")
    chip, core = side // 2, side % 2
    partner = chip * 2 + 1 - core
    across = (1 - chip) * 2 + core
    barrier = pltpu.get_barrier_semaphore()
    for k in range(1, 4):
        pl.semaphore_signal(barrier, inc=1, device_id={"tp": (side + k) % 4}, device_id_type=MESH)
    pl.semaphore_wait(barrier, 3)
    rows = parts_ref.shape[1] // chunks

    def core_copy(far, chunk):
        chip_to = far * (1 - chip) + (1 - far) * chip
        part = pl.ds(chunk * rows, rows)
        return pltpu.make_async_remote_copy(
            src_ref=parts_ref.at[chip_to * 2 + 1 - core, part],
            dst_ref=core_in.at[far, part],
            send_sem=core_sems.at[0, far, chunk],
            recv_sem=core_sems.at[1, far, chunk],
            device_id={"tp": partner},
            device_id_type=MESH,
        )

    to_core = {}
    for far in (1, 0):
        for chunk in range(chunks):
            to_core[far, chunk] = core_copy(far, chunk)
            to_core[far, chunk].start()
    to_all = []
    for k in range(1, 4):
        copy = pltpu.make_async_remote_copy(
            src_ref=small_ref,
            dst_ref=small_in.at[side],
            send_sem=small_sems.at[0, k],
            recv_sem=small_sems.at[1, k],
            device_id={"tp": (side + k) % 4},
            device_id_type=MESH,
        )
        copy.start()
        to_all.append(copy)
    small_in[side] = small_ref[...]
    to_across = []
    for chunk in range(chunks):
        part = pl.ds(chunk * rows, rows)
        to_core[1, chunk].wait_recv()
        staged[part, :] = (
            parts_ref[across, part, :].astype(jnp.float32)
            + core_in[1, part, :].astype(jnp.float32)
        ).astype(jnp.bfloat16)
        copy = pltpu.make_async_remote_copy(
            src_ref=staged.at[part],
            dst_ref=cross_in.at[part],
            send_sem=cross_sems.at[0, chunk],
            recv_sem=cross_sems.at[1, chunk],
            device_id={"tp": across},
            device_id_type=MESH,
        )
        copy.start()
        to_across.append(copy)
    for chunk in range(chunks):
        part = pl.ds(chunk * rows, rows)
        to_core[0, chunk].wait_recv()
        out_ref[part, :] = parts_ref[side, part, :].astype(jnp.float32) + core_in[
            0, part, :
        ].astype(jnp.float32)
    for copy in to_all:
        copy.wait_recv()
    small_out[...] = (small_in[0] + small_in[1]) + (small_in[2] + small_in[3])
    for chunk in range(chunks):
        part = pl.ds(chunk * rows, rows)
        to_across[chunk].wait_recv()
        out_ref[part, :] = out_ref[part, :] + cross_in[part, :].astype(jnp.float32)
    for copy in list(to_core.values()) + to_all + to_across:
        copy.wait_send()


def share_sums(parts, small, collective_id):
    sharers = lax.axis_size("tp")
    _, count, share = parts.shape
    if sharers != 4 or count % 64:
        mine = lax.psum_scatter(parts, "tp", scatter_dimension=0, tiled=False)
        return mine.astype(jnp.float32), lax.psum(small, "tp")
    width = small.shape[1]
    lanes = -(-width // 128) * 128
    small = jnp.pad(small, ((0, 0), (0, lanes - width)))
    chunks = 4
    mine, small = pl.pallas_call(
        functools.partial(share_kernel, chunks),
        out_shape=[
            jax.ShapeDtypeStruct((count, share), jnp.float32),
            jax.ShapeDtypeStruct((count, lanes), jnp.float32),
        ],
        in_specs=[pl.BlockSpec(memory_space=pltpu.VMEM)] * 2,
        out_specs=[pl.BlockSpec(memory_space=pltpu.VMEM)] * 2,
        scratch_shapes=[
            pltpu.VMEM((2, count, share), jnp.bfloat16),
            pltpu.VMEM((count, share), jnp.bfloat16),
            pltpu.VMEM((count, share), jnp.bfloat16),
            pltpu.VMEM((sharers, count, lanes), jnp.float32),
            pltpu.SemaphoreType.DMA((2, 2, chunks)),
            pltpu.SemaphoreType.DMA((2, chunks)),
            pltpu.SemaphoreType.DMA((2, sharers)),
        ],
        compiler_params=pltpu.CompilerParams(collective_id=collective_id, has_side_effects=True),
    )(parts, small)
    return mine, small[:, :width]


def dequantize(codes, scodes, second, row_start):
    height, width = codes.shape
    levels = jnp.zeros(codes.shape, jnp.float32)
    for level in range(16):
        levels = jnp.where(codes == level, jnp.float32(NORMAL_FLOAT[level]), levels)
    group_ids = (row_start + jnp.arange(height, dtype=jnp.int32)) // QGROUP
    group_list = jnp.arange(second.shape[0], dtype=jnp.int32)
    picker = (group_ids[:, None] == group_list[None, :]).astype(jnp.float32)
    second_rows = jnp.dot(picker, second, precision=lax.Precision.HIGHEST)
    absmax = second_rows * ((scodes.astype(jnp.float32) + 1.0) / 256.0)
    scaled = levels.reshape(height, width // QBLOCK, QBLOCK) * absmax[:, :, None]
    return scaled.reshape(height, width).astype(jnp.bfloat16)


def rope_tables(positions):
    half = HEAD_SIZE // 2
    exponent = jnp.arange(half, dtype=jnp.float32) * (2.0 / HEAD_SIZE)
    frequency = jnp.power(jnp.float32(ROPE_BASE), -exponent)
    angle = positions.astype(jnp.float32)[:, None] * frequency[None, :]
    return (jnp.cos(angle), jnp.sin(angle))


def rotate(heads, cosine, sine):
    half = heads.shape[-1] // 2
    first = heads[..., :half]
    second = heads[..., half:]
    across = cosine[:, None, :]
    along = sine[:, None, :]
    return jnp.concatenate(
        [first * across - second * along, second * across + first * along], axis=-1
    )


def unrotate(grad, cosine, sine):
    half = grad.shape[-1] // 2
    first = grad[..., :half]
    second = grad[..., half:]
    across = cosine[:, None, :]
    along = sine[:, None, :]
    return jnp.concatenate(
        [first * across + second * along, second * across - first * along], axis=-1
    )


def head_norm(heads, gain):
    scale = lax.rsqrt(jnp.mean(heads * heads, axis=-1, keepdims=True) + EPSILON)
    return (heads * scale * gain, scale)


def head_norm_back(heads, scale, gain, grad):
    weighted = grad * gain
    inner = jnp.mean(weighted * heads, axis=-1, keepdims=True)
    return scale * weighted - scale**3 * heads * inner


def probabilities(q_rot, keys, query_pos, key_pos):
    count, q_heads, width = q_rot.shape
    kv_heads = keys.shape[1]
    grouped = q_rot.reshape(count, kv_heads, q_heads // kv_heads, width)
    scores = (
        jnp.einsum("tkgd,lkd->kgtl", grouped, keys, preferred_element_type=jnp.float32)
        * SCORE_SCALE
    )
    gap = query_pos[:, None] - key_pos[None, :]
    allowed = (gap >= 0) & (gap < WINDOW_TOKENS) & (key_pos[None, :] >= 0)
    weights = jnp.where(allowed, jnp.exp(scores), 0.0)
    return (weights / jnp.sum(weights, axis=-1, keepdims=True), grouped)


def attention_forward(q_rot, keys, values, query_pos, key_pos):
    count, q_heads, width = q_rot.shape
    probability, grouped = probabilities(q_rot, keys, query_pos, key_pos)
    prob_low = probability.astype(jnp.bfloat16)
    mixed = jnp.einsum("kgtl,lkd->tkgd", prob_low, values, preferred_element_type=jnp.float32)
    return mixed.reshape(count, q_heads * width).astype(jnp.bfloat16)


def attention_backward(q_rot, keys, values, output_gradient, query_pos, key_pos):
    count, q_heads, width = q_rot.shape
    kv_heads = keys.shape[1]
    probability, grouped = probabilities(q_rot, keys, query_pos, key_pos)
    prob_low = probability.astype(jnp.bfloat16)
    grad_grouped = output_gradient.reshape(count, kv_heads, q_heads // kv_heads, width)
    grad_prob = jnp.einsum(
        "tkgd,lkd->kgtl", grad_grouped, values, preferred_element_type=jnp.float32
    )
    grad_values = jnp.einsum(
        "kgtl,tkgd->lkd", prob_low, grad_grouped, preferred_element_type=jnp.float32
    )
    inner = jnp.sum(probability * grad_prob, axis=-1, keepdims=True)
    grad_scores = (probability * (grad_prob - inner) * SCORE_SCALE).astype(jnp.bfloat16)
    grad_query = jnp.einsum(
        "kgtl,lkd->tkgd", grad_scores, keys, preferred_element_type=jnp.float32
    ).reshape(count, q_heads, width)
    grad_keys = jnp.einsum(
        "kgtl,tkgd->lkd", grad_scores, grouped, preferred_element_type=jnp.float32
    )
    return (grad_query, grad_keys, grad_values)


def on_device(
    tokens,
    out_grad,
    in_gain,
    query_gain,
    key_gain,
    post_gain,
    q_codes,
    q_scodes,
    q_second,
    kv_codes,
    kv_scodes,
    kv_second,
    o_codes,
    o_scodes,
    o_second,
    q_down,
    query_up,
    kv_down,
    key_value_up,
    output_down,
    output_up,
):
    count = tokens.shape[0]
    share = tokens.shape[1]
    ctx_rank = lax.axis_index("ctx")
    tp_rank = lax.axis_index("tp")
    column_start = tp_rank * share
    row_start = ctx_rank * q_codes.shape[0]
    q_width = query_up.shape[1]
    kv_width = key_value_up.shape[2]
    q_heads_here = q_width // HEAD_SIZE
    kv_heads_here = kv_width // HEAD_SIZE
    q_part = dequantize(q_codes, q_scodes, q_second, row_start)
    k_part = dequantize(kv_codes[0], kv_scodes[0], kv_second[0], row_start)
    v_part = dequantize(kv_codes[1], kv_scodes[1], kv_second[1], row_start)
    o_part = dequantize(o_codes, o_scodes, o_second, row_start)
    key_matrix, value_matrix = gather_pair(k_part, v_part, 1)
    q_part, o_part, key_matrix, value_matrix = lax.optimization_barrier(
        (q_part, o_part, key_matrix, value_matrix)
    )
    query_matrix, output_matrix = gather_pair(q_part, o_part, 2)
    whole_tokens = lax.all_gather(tokens, "tp", axis=1, tiled=True)
    wide = whole_tokens.astype(jnp.float32)
    row_scale = lax.rsqrt(jnp.mean(wide * wide, axis=1, keepdims=True) + EPSILON)
    normalized_input = (wide * row_scale * in_gain).astype(jnp.bfloat16)
    query_lowrank = jnp.dot(normalized_input, q_down, preferred_element_type=jnp.float32).astype(
        jnp.bfloat16
    )
    key_lowrank = jnp.dot(normalized_input, kv_down[0], preferred_element_type=jnp.float32).astype(
        jnp.bfloat16
    )
    value_lowrank = jnp.dot(
        normalized_input, kv_down[1], preferred_element_type=jnp.float32
    ).astype(jnp.bfloat16)
    query_rows = jnp.dot(
        normalized_input, query_matrix, preferred_element_type=jnp.float32
    ) + ADAPTER_SCALE * jnp.dot(query_lowrank, query_up, preferred_element_type=jnp.float32)
    key = jnp.dot(
        normalized_input, key_matrix, preferred_element_type=jnp.float32
    ) + ADAPTER_SCALE * jnp.dot(key_lowrank, key_value_up[0], preferred_element_type=jnp.float32)
    value_total = jnp.dot(
        normalized_input, value_matrix, preferred_element_type=jnp.float32
    ) + ADAPTER_SCALE * jnp.dot(value_lowrank, key_value_up[1], preferred_element_type=jnp.float32)
    value_rows = value_total.astype(jnp.bfloat16)
    query_pos = ctx_rank * count + jnp.arange(count, dtype=jnp.int32)
    key_pos = ctx_rank * count - WINDOW_TOKENS + jnp.arange(WINDOW_TOKENS + count, dtype=jnp.int32)
    cosine, sine = rope_tables(query_pos)
    q_heads = query_rows.reshape(count, q_heads_here, HEAD_SIZE)
    q_normed, q_scale = head_norm(q_heads, query_gain)
    q_rot = rotate(q_normed, cosine, sine).astype(jnp.bfloat16)
    key_head_rows = key.reshape(count, kv_heads_here, HEAD_SIZE)
    k_normed, k_scale = head_norm(key_head_rows, key_gain)
    k_rot = rotate(k_normed, cosine, sine).astype(jnp.bfloat16)
    piece_rows = min(WINDOW_TOKENS, count)
    pieces = WINDOW_TOKENS // piece_rows
    stacked = jnp.stack([k_rot.reshape(count, kv_width), value_rows])
    arrived = []
    for offset in range(pieces, 0, -1):
        arrived.append(from_behind(stacked, "ctx", offset))
    window = jnp.concatenate(arrived + [stacked], axis=1)
    window_keys = window[0].reshape(WINDOW_TOKENS + count, kv_heads_here, HEAD_SIZE)
    window_values = window[1].reshape(WINDOW_TOKENS + count, kv_heads_here, HEAD_SIZE)
    attended_rows = attention_forward(q_rot, window_keys, window_values, query_pos, key_pos)
    low_part = jnp.dot(attended_rows, output_down, preferred_element_type=jnp.float32)
    sharers = lax.axis_size("tp")
    out_part = jnp.stack(
        [
            jnp.dot(
                attended_rows,
                output_matrix[k * share : (k + 1) * share].T,
                preferred_element_type=jnp.float32,
            ).astype(jnp.bfloat16)
            for k in range(sharers)
        ]
    )
    out_mine, low_sum = share_sums(out_part, low_part, 4)
    gain_mine = lax.dynamic_slice_in_dim(post_gain, column_start, share, 0)
    output_lowrank = low_sum.astype(jnp.bfloat16)
    up_mine = lax.dynamic_slice_in_dim(output_up, column_start, share, 1)
    out_mine = out_mine + ADAPTER_SCALE * jnp.dot(output_lowrank, up_mine, preferred_element_type=jnp.float32)
    square_sum = lax.psum(jnp.sum(out_mine * out_mine, axis=1, keepdims=True), "tp")
    out_scale = lax.rsqrt(square_sum / D + EPSILON)
    mixed = (tokens.astype(jnp.float32) + out_mine * out_scale * gain_mine).astype(jnp.bfloat16)
    weighted_out = out_grad.astype(jnp.float32) * gain_mine
    out_inner = lax.psum(jnp.sum(weighted_out * out_mine, axis=1, keepdims=True), "tp") / D
    grad_mine = (out_scale * weighted_out - out_scale**3 * out_mine * out_inner).astype(
        jnp.bfloat16
    )
    output_gradient = lax.all_gather(grad_mine, "tp", axis=1, tiled=True)
    output_mixture = jnp.dot(
        output_gradient, output_up.T, preferred_element_type=jnp.float32
    ).astype(jnp.bfloat16)
    output_up_part = jnp.dot(output_lowrank.T, grad_mine, preferred_element_type=jnp.float32)
    output_down_part = jnp.dot(
        output_mixture.T, attended_rows, preferred_element_type=jnp.float32
    )
    attended_gradient = (
        jnp.dot(output_gradient, output_matrix, preferred_element_type=jnp.float32)
        + ADAPTER_SCALE * jnp.dot(output_mixture, output_down.T, preferred_element_type=jnp.float32)
    ).astype(jnp.bfloat16)
    query_grad, key_window_grad, value_window_grad = attention_backward(
        q_rot, window_keys, window_values, attended_gradient, query_pos, key_pos
    )
    window_grad = jnp.stack(
        [
            key_window_grad.reshape(WINDOW_TOKENS + count, kv_width),
            value_window_grad.reshape(WINDOW_TOKENS + count, kv_width),
        ]
    )
    front_rows = window_grad[:, :WINDOW_TOKENS].astype(jnp.bfloat16)
    own = window_grad[:, WINDOW_TOKENS:]
    returned = jnp.zeros((2, piece_rows, kv_width), jnp.float32)
    for offset in range(1, pieces + 1):
        piece = front_rows[:, (pieces - offset) * piece_rows : (pieces - offset + 1) * piece_rows]
        returned = returned + from_behind(piece, "ctx", -offset).astype(jnp.float32)
    own = jnp.concatenate([own[:, : count - piece_rows], own + returned], axis=1)
    q_norm_grad = unrotate(query_grad, cosine, sine)
    k_norm_grad = unrotate(own[0].reshape(count, kv_heads_here, HEAD_SIZE), cosine, sine)
    query_gradient_lowrank = (
        head_norm_back(q_heads, q_scale, query_gain, q_norm_grad)
        .reshape(count, q_width)
        .astype(jnp.bfloat16)
    )
    key_gradient_lowrank = (
        head_norm_back(key_head_rows, k_scale, key_gain, k_norm_grad)
        .reshape(count, kv_width)
        .astype(jnp.bfloat16)
    )
    value_gradient_lowrank = own[1].astype(jnp.bfloat16)
    query_mixture = jnp.dot(query_gradient_lowrank, query_up.T, preferred_element_type=jnp.float32)
    key_mixture = jnp.dot(
        key_gradient_lowrank, key_value_up[0].T, preferred_element_type=jnp.float32
    )
    value_mixture = jnp.dot(
        value_gradient_lowrank, key_value_up[1].T, preferred_element_type=jnp.float32
    )
    into_part = jnp.dot(query_gradient_lowrank, query_matrix.T, preferred_element_type=jnp.float32)
    into_part = into_part + jnp.dot(
        key_gradient_lowrank, key_matrix.T, preferred_element_type=jnp.float32
    )
    into_part = into_part + jnp.dot(
        value_gradient_lowrank, value_matrix.T, preferred_element_type=jnp.float32
    )
    query_mixture, key_mixture, value_mixture = lax.psum(
        (query_mixture, key_mixture, value_mixture), "tp"
    )
    query_mixture = query_mixture.astype(jnp.bfloat16)
    key_mixture = key_mixture.astype(jnp.bfloat16)
    value_mixture = value_mixture.astype(jnp.bfloat16)
    into_mine = lax.psum_scatter(
        into_part.astype(jnp.bfloat16), "tp", scatter_dimension=1, tiled=True
    ).astype(jnp.float32)
    q_down_mine = lax.dynamic_slice_in_dim(q_down, column_start, share, 0)
    k_down_mine = lax.dynamic_slice_in_dim(kv_down[0], column_start, share, 0)
    v_down_mine = lax.dynamic_slice_in_dim(kv_down[1], column_start, share, 0)
    adapter_term = (
        jnp.dot(query_mixture, q_down_mine.T, preferred_element_type=jnp.float32)
        + jnp.dot(key_mixture, k_down_mine.T, preferred_element_type=jnp.float32)
        + jnp.dot(value_mixture, v_down_mine.T, preferred_element_type=jnp.float32)
    )
    normalized_gradient = into_mine + ADAPTER_SCALE * adapter_term
    in_gain_mine = lax.dynamic_slice_in_dim(in_gain, column_start, share, 0)
    weighted_in = normalized_gradient * in_gain_mine
    wide_mine = tokens.astype(jnp.float32)
    in_inner = lax.psum(jnp.sum(weighted_in * wide_mine, axis=1, keepdims=True), "tp") / D
    tokens_grad = (
        out_grad.astype(jnp.float32) + row_scale * weighted_in - row_scale**3 * wide_mine * in_inner
    )
    in_projection = float(D) ** 0.5 * row_scale * in_inner
    normed_mine = (wide_mine * row_scale * in_gain_mine).astype(jnp.bfloat16)
    mixtures = jnp.concatenate([query_mixture, key_mixture, value_mixture], axis=1)
    down_part = jnp.concatenate(
        [jnp.dot(mixtures.T, normed_mine, preferred_element_type=jnp.float32), output_up_part]
    )
    up_part = jnp.concatenate(
        [
            jnp.dot(query_lowrank.T, query_gradient_lowrank, preferred_element_type=jnp.float32),
            jnp.dot(key_lowrank.T, key_gradient_lowrank, preferred_element_type=jnp.float32),
            jnp.dot(value_lowrank.T, value_gradient_lowrank, preferred_element_type=jnp.float32),
            output_down_part,
        ],
        axis=1,
    )
    down_sum, up_sum = reduce_gradients(ADAPTER_SCALE * down_part, ADAPTER_SCALE * up_part, 3)
    rank = query_up.shape[0]
    down_sum = down_sum.reshape(sharers, 4, rank, share)
    down_turned = down_sum[:, :3].transpose(1, 0, 3, 2).reshape(3, sharers * share, rank)
    query_down_gradient = down_turned[0]
    key_value_down_gradient = down_turned[1:]
    output_up_gradient = down_sum[:, 3].transpose(1, 0, 2).reshape(rank, sharers * share)
    query_up_gradient = up_sum[:, :q_width]
    key_value_up_gradient = jnp.stack(
        [
            up_sum[:, q_width : q_width + kv_width],
            up_sum[:, q_width + kv_width : q_width + 2 * kv_width],
        ]
    )
    output_down_gradient = up_sum[:, q_width + 2 * kv_width :].T
    return (
        mixed,
        tokens_grad,
        query_down_gradient,
        query_up_gradient,
        key_value_down_gradient,
        key_value_up_gradient,
        output_down_gradient,
        output_up_gradient,
        in_projection,
    )


def solution(mesh):
    placed = (
        P("ctx", "tp"),
        P("ctx", "tp"),
        P(),
        P(),
        P(),
        P(),
        P("ctx", "tp"),
        P("ctx", "tp"),
        P(None, "tp"),
        P(None, "ctx", "tp"),
        P(None, "ctx", "tp"),
        P(None, None, "tp"),
        P("ctx", "tp"),
        P("ctx", "tp"),
        P(None, "tp"),
        P(),
        P(None, "tp"),
        P(),
        P(None, None, "tp"),
        P("tp", None),
        P(),
    )
    return jax.shard_map(
        on_device,
        mesh=mesh,
        in_specs=placed,
        out_specs=(
            P("ctx", "tp"),
            P("ctx", "tp"),
            P(),
            P(None, "tp"),
            P(),
            P(None, None, "tp"),
            P("tp", None),
            P(),
            P("ctx", None),
        ),
        check_vma=False,
    )
```
